512 devices in a mesh: screen: 16 (over z, core), depth: 32 (over y, x).
Axes of the slice: x: 4, y: 8, z: 8, core: 2. Of those that a mesh axis runs over, the one named last changes fastest.
Arguments:
- density: bfloat16 [256, 256, 2048], P('depth', None, 'screen'), as said below
- bin_index: int32 [256, 256, 2048], P('depth', None, 'screen'), may hold values from 0 to 255
- transfer: bfloat16 [4, 256], replicated, may hold values from 0.049804688 to 1
- view_side: int32 [2048], P('screen'), may hold values 0 or 1
Outputs:
- image: float32 [4, 256, 2048], P(None, 'depth', 'screen')
The draws below stay inside these ranges and needn't reach their ends.
Inputs may be any that keep to these rules, and one draw needn't show every extreme that they name: Up to bfloat16 rounding a voxel's density lies between bin_index / 256 and (bin_index + 1) / 256.
All inputs are finite; a program needn't handle non-finite values. No bound on the sum of `view_side` on one device may be relied on, other than what follows from the above.
Results may differ from the reference program's by a relative error of at most 0.0003.
Values may be sent and summed in bfloat16 or wider, within the bound.
No kernel may reach another device: no remote copies, remote signals or barrier semaphores. Data moves between devices by JAX's collectives and lax.ppermute only.
A program may use at most 64 MiB of HBM per device.

```python
import jax
import jax.numpy as jnp
from jax import lax

BINS = 256
COL_DEV = 128
COLS = 2048
ROWS = 256
DEPTH = 256
N_SCREEN = 16


def bin_field(key):
    return jax.random.randint(jax.random.fold_in(key, 11), (DEPTH, ROWS, COLS), 0, BINS, dtype=jnp.int32)


def draw_bin_index(key, part):
    return bin_field(key)


def draw_density(key, part):
    levels = bin_field(key).astype(jnp.float32)
    fraction = jax.random.uniform(jax.random.fold_in(key, 12), (DEPTH, ROWS, COLS), jnp.float32)
    fraction = fraction * 0.98
    return ((levels + fraction) / BINS).astype(jnp.bfloat16)


def plant(values, own_key, smallest, largest):
    place = [jax.random.randint(jax.random.fold_in(own_key, axis), (), 0, length) for axis, length in enumerate(values.shape)]
    longest = values.shape.index(max(values.shape))
    neighbour = place[:longest] + [(place[longest] + 1) % values.shape[longest]] + place[longest + 1:]
    return values.at[tuple(place)].set(smallest).at[tuple(neighbour)].set(largest)


def setup_inputs(seed: int = 0) -> dict:
    seeds = jax.random.split(jax.random.key(seed), 5)
    density = draw_density(jax.random.fold_in(seeds[4], 71), 0)
    bin_index = draw_bin_index(jax.random.fold_in(seeds[4], 71), 0)
    transfer = jnp.clip(jax.random.uniform(seeds[2], (4, BINS), jnp.float32, 0.049804688, 1.0), 0.049804688, 1.0).astype(jnp.bfloat16)
    view_side = plant((jax.random.randint(seeds[3], (COLS,), 0, 2) < 1).astype(jnp.int32), jax.random.fold_in(seeds[3], 1), 0, 1)
    return dict(density=density, bin_index=bin_index, transfer=transfer, view_side=view_side)


LIGHT_DIRECTION = (0.36, 0.48, 0.8)
AMBIENT = 0.3
DIFFUSE = 0.7
OPTICAL = 4.0

def centred_diff(field, axis):
    length = field.shape[axis] - 4

    def shifted(offset):
        return lax.slice_in_dim(field, 2 + offset, 2 + offset + length, axis=axis)
    return (8.0 * (shifted(1) - shifted(-1)) - (shifted(2) - shifted(-2))) / 12.0

def shading_of(padded):
    field = padded.astype(jnp.float32)
    grad_depth = centred_diff(field[:, 2:-2, 2:-2], 0)
    grad_rows = centred_diff(field[2:-2, :, 2:-2], 1)
    grad_cols = centred_diff(field[2:-2, 2:-2, :], 2)
    light_dot = LIGHT_DIRECTION[0] * grad_cols + LIGHT_DIRECTION[1] * grad_rows + LIGHT_DIRECTION[2] * grad_depth
    squared = grad_cols * grad_cols + grad_rows * grad_rows + grad_depth * grad_depth
    return AMBIENT + DIFFUSE * jnp.abs(light_dot) / jnp.sqrt(squared + 1.0)

def render(padded, bin_block, side_block, transfer):
    shading = shading_of(padded)
    table = transfer.astype(jnp.float32)
    extinction = table[3][bin_block]
    optical = extinction * (OPTICAL / DEPTH)
    opacity = 1.0 - jnp.exp(-optical)
    running = jnp.cumsum(optical, axis=0)
    through = running[-1]
    before = jnp.where(side_block == 0, running - optical, through[None] - running)
    weight = jnp.exp(-before) * opacity * shading
    channels = []
    for channel in range(3):
        emission = table[channel][bin_block]
        channels.append(lax.optimization_barrier(jnp.sum(emission * weight, axis=0)))
    channels.append(1.0 - jnp.exp(-through))
    return jnp.stack(channels, axis=0)

def reference(density, bin_index, transfer, view_side):
    padded_all = jnp.pad(density, 2)

    def column_part(index):
        offset = (index * COL_DEV).astype(jnp.int32)
        padded = lax.dynamic_slice_in_dim(padded_all, offset, COL_DEV + 4, axis=2)
        bin_block = lax.dynamic_slice_in_dim(bin_index, offset, COL_DEV, axis=2)
        side_block = lax.dynamic_slice_in_dim(view_side, offset, COL_DEV, axis=0)
        return render(padded, bin_block, side_block, transfer)
    pieces = lax.map(column_part, jnp.arange(N_SCREEN, dtype=jnp.int32))
    return jnp.transpose(pieces, (1, 2, 0, 3)).reshape(4, ROWS, COLS)
```

```python
import jax
import jax.numpy as jnp
from jax import lax
from jax.experimental import pallas as pl
from jax.experimental.pallas import tpu as pltpu
from jax.sharding import PartitionSpec as P
import math

LIGHT_DIRECTION = (0.36, 0.48, 0.8)
AMBIENT = 0.3
DIFFUSE = 0.7
OPTICAL = 4.0
LEAST = 0.049804688
UNIT = 4096.0
CODES = 65535.0

F32, BF16, I32 = jnp.float32, jnp.bfloat16, jnp.int32


def stencil(offset):
    one = jnp.where(offset > 0, 8.0, -8.0)
    two = jnp.where(offset > 0, -1.0, 1.0)
    far = jnp.abs(offset)
    return jnp.where(far == 1, one, jnp.where(far == 2, two, 0.0)).astype(BF16)


def iota(shape, dim):
    return lax.broadcasted_iota(I32, shape, dim)


def colour_code(layers, depth_total):
    step = OPTICAL / depth_total
    low = LEAST * AMBIENT * -math.expm1(-layers * LEAST * step) * 0.999
    high = -math.expm1(-layers * step) * 1.001
    return math.log(low), math.log(high / low) / CODES


def edges_kernel(x_ref, cols_ref, first_ref, last_ref):
    layers, _, cols = x_ref.shape
    k, lane = iota((layers * cols, cols), 0), iota((layers * cols, cols), 1)
    j = lane & 3
    column = (lane >> 2) * cols + jnp.where(j < 2, j, cols - 4 + j)
    pick = jnp.where(k == column, 1.0, 0.0).astype(BF16)
    x = jnp.concatenate([x_ref[d] for d in range(layers)], axis=1)
    cols_ref[...] = jnp.dot(x, pick, preferred_element_type=F32).astype(BF16)
    first_ref[...] = x_ref[:2]
    last_ref[...] = x_ref[layers - 2 :]


def brick_kernel(depth_total, x_ref, before_ref, after_ref, left_ref, right_ref, bins_ref, table_ref, side_ref, out_ref, gc_ref, gr_ref):
    layers, rows, cols = x_ref.shape
    lane = iota((rows, cols), 1)
    halo = jnp.where((lane & 2) == 0, right_ref[...], left_ref[...])
    k, c = iota((cols, cols), 0), iota((cols, cols), 1)
    inner = stencil(k - c)
    j = k & 3
    place = jnp.where(j < 2, cols + j, j - 4)
    outer = stencil(place - c)
    across = stencil(iota((rows, rows), 1) - iota((rows, rows), 0))
    for d in range(layers):
        x = x_ref[d]
        edge = jnp.where((k >> 2) == d, outer, jnp.zeros_like(outer))
        gc_ref[d] = jnp.dot(
            jnp.concatenate([x, halo], axis=1), jnp.concatenate([inner, edge], axis=0), preferred_element_type=F32
        )
        gr_ref[d] = jnp.dot(across, x, preferred_element_type=F32)
    table = table_ref[...].astype(F32)
    step = OPTICAL / depth_total
    extinct = table[3:4]
    opacity = 1.0 - jnp.exp(-(extinct * step))
    half = 128
    wide = [table[i : i + 1] * opacity for i in range(3)] + [extinct]
    tabs = [[jnp.broadcast_to(w[:, h * half : (h + 1) * half], (8, half)) for h in range(2)] for w in wide]
    far_side = jnp.broadcast_to(side_ref[...], (8, cols)) != 0
    low, unit = colour_code(layers, depth_total)

    def layer(d, at):
        if d < 2:
            return before_ref[d, at]
        if d >= layers + 2:
            return after_ref[d - layers - 2, at]
        return x_ref[d - 2, at]

    def block(b, carry):
        at = pl.ds(pl.multiple_of(b * 16, 16), 16)
        f = [layer(d, at).astype(F32) for d in range(layers + 4)]
        for h in range(2):
            at8 = pl.ds(pl.multiple_of(b * 16 + h * 8, 8), 8)
            rows8 = slice(h * 8, h * 8 + 8)
            colour = [jnp.zeros((8, cols), F32)] * 3
            clear = jnp.ones((8, cols), F32)
            total = jnp.zeros((8, cols), F32)
            for d in range(layers):
                gd = 8.0 * (f[d + 3][rows8] - f[d + 1][rows8]) - (f[d + 4][rows8] - f[d][rows8])
                gc, gr = gc_ref[d, at8], gr_ref[d, at8]
                light = LIGHT_DIRECTION[0] * gc + LIGHT_DIRECTION[1] * gr + LIGHT_DIRECTION[2] * gd
                norm = lax.rsqrt(gc * gc + gr * gr + gd * gd + 144.0)
                shade = AMBIENT + DIFFUSE * jnp.abs(light) * norm
                index = bins_ref[d, at8]
                upper = index >= half
                index = index & (half - 1)
                looked = [
                    jnp.where(
                        upper,
                        jnp.take_along_axis(t[1], index, axis=1, mode="promise_in_bounds"),
                        jnp.take_along_axis(t[0], index, axis=1, mode="promise_in_bounds"),
                    )
                    for t in tabs
                ]
                through = jnp.exp(looked[3] * -step)
                total = total + looked[3]
                keep = jnp.where(far_side, through, 1.0)
                scale = jnp.where(far_side, 1.0, clear) * shade
                colour = [colour[i] * keep + looked[i] * scale for i in range(3)]
                clear = clear * through
            code = [
                jnp.clip((jnp.log(v) - low) * (1.0 / unit) + 0.5, 0.0, CODES).astype(I32) for v in colour
            ]
            count = (total * UNIT + 0.5).astype(I32)
            at_out = b * 2 + h
            out_ref[at_out, 0:8, :] = code[0] + (code[1] << 16)
            out_ref[at_out, 8:16, :] = code[2] + (count << 16)
        return carry

    lax.fori_loop(0, rows // 16, block, 0)


def merge_kernel(layers, depth_total, in_ref, side_ref, out_ref):
    parts, _, cols = in_ref.shape
    step = OPTICAL / depth_total / UNIT
    low, unit = colour_code(layers, depth_total)
    far_side = jnp.broadcast_to(side_ref[...], (8, cols)) != 0
    counts = [lax.shift_right_logical(in_ref[p, 8:16, :], 16) for p in range(parts)]
    total = counts[0]
    for v in counts[1:]:
        total = total + v
    ahead = jnp.where(far_side, total, 0)
    colour = [jnp.zeros((8, cols), F32)] * 3
    for p in range(parts):
        first, second = in_ref[p, 0:8, :], in_ref[p, 8:16, :]
        codes = [first & 0xFFFF, lax.shift_right_logical(first, 16), second & 0xFFFF]
        behind = ahead - counts[p]
        shift = jnp.where(far_side, behind, ahead).astype(F32) * -step + low
        colour = [colour[i] + jnp.exp(codes[i].astype(F32) * unit + shift) for i in range(3)]
        ahead = jnp.where(far_side, behind, ahead + counts[p])
    for i in range(3):
        out_ref[i] = colour[i]
    out_ref[3] = 1.0 - jnp.exp(total.astype(F32) * -step)


def shift(x, axis, up):
    pairs = [(i, i + 1) for i in range(lax.axis_size(axis) - 1)]
    return lax.ppermute(x, axis, pairs if up else [(b, a) for a, b in pairs])


def on_device(density, bin_index, transfer, view_side):
    layers, rows, cols = density.shape
    count = lax.axis_size("depth")
    depth_total = layers * count
    block_rows = rows // count
    edge = jax.ShapeDtypeStruct((2, rows, cols), BF16)
    columns, first, last = pl.pallas_call(
        edges_kernel, out_shape=(jax.ShapeDtypeStruct((rows, cols), BF16), edge, edge), name="edges"
    )(density)
    before = shift(last, "depth", True)
    after = shift(first, "depth", False)
    left = shift(columns, "screen", True)
    right = shift(columns, "screen", False)
    side = view_side.reshape(1, cols)
    tiles = pl.pallas_call(
        lambda *refs: brick_kernel(depth_total, *refs),
        out_shape=jax.ShapeDtypeStruct((count, 2 * block_rows, cols), I32),
        scratch_shapes=[pltpu.VMEM((layers, rows, cols), F32)] * 2,
        name="brick",
    )(density, before, after, left, right, bin_index, transfer, side)
    arrived = lax.all_to_all(tiles, "depth", split_axis=0, concat_axis=0, tiled=True)
    return pl.pallas_call(
        lambda *refs: merge_kernel(layers, depth_total, *refs),
        out_shape=jax.ShapeDtypeStruct((4, block_rows, cols), F32),
        name="merge",
    )(arrived, side)


def solution(mesh):
    placed = (P("depth", None, "screen"), P("depth", None, "screen"), P(), P("screen"))
    return jax.shard_map(
        on_device, mesh=mesh, in_specs=placed, out_specs=P(None, "depth", "screen"), check_vma=False
    )
```

```python
import jax
import jax.numpy as jnp
from jax import lax
from jax.experimental import pallas as pl
from jax.experimental.pallas import tpu as pltpu
from jax.sharding import PartitionSpec as P
import math

LIGHT_DIRECTION = (0.36, 0.48, 0.8)
AMBIENT = 0.3
DIFFUSE = 0.7
OPTICAL = 4.0
LEAST = 0.049804688
UNIT = 4096.0
CODES = 65535.0
GROUP = 2
HALF = 128
PAIR = 4096.0
MIDDLE = 2150.0
ROUND = 1.5 * 2.0**23 * PAIR

F32, BF16, I32 = jnp.float32, jnp.bfloat16, jnp.int32


def stencil(offset):
    one = jnp.where(offset > 0, 8.0, -8.0)
    two = jnp.where(offset > 0, -1.0, 1.0)
    far = jnp.abs(offset)
    return jnp.where(far == 1, one, jnp.where(far == 2, two, 0.0)).astype(BF16)


def iota(shape, dim):
    return lax.broadcasted_iota(I32, shape, dim)


def colour_code(layers, depth_total):
    step = OPTICAL / depth_total
    low = LEAST * AMBIENT * -math.expm1(-layers * LEAST * step) * 0.999
    high = -math.expm1(-layers * step) * 1.001
    return math.log(low), math.log(high / low) / CODES


def lanes(table, index):
    numbers = lax.GatherDimensionNumbers((), (1,), (1,), (0,), (0,))
    return lax.gather(
        table, index[..., None], numbers, (1, 1), mode=lax.GatherScatterMode.PROMISE_IN_BOUNDS
    )


def faces_kernel(x_hbm, first_ref, last_ref, sems):
    layers = x_hbm.shape[0]
    here, count = lax.axis_index("depth"), lax.axis_size("depth")
    copies = [
        pltpu.make_async_copy(x_hbm.at[pl.ds(start, 2)], ref, sems.at[i])
        for i, (start, ref) in enumerate([(0, first_ref), (layers - 2, last_ref)])
    ]
    for copy in copies:
        copy.start()
    for copy in copies:
        copy.wait()

    @pl.when(here == 0)
    def _():
        first_ref[...] = jnp.zeros_like(first_ref)

    @pl.when(here == count - 1)
    def _():
        last_ref[...] = jnp.zeros_like(last_ref)


def columns_kernel(x_ref, cols_ref):
    layers, _, cols = x_ref.shape
    here, count = lax.axis_index("screen"), lax.axis_size("screen")
    k = iota((layers * cols, cols), 0)
    j = iota((1, cols), 1) & 3
    low, high = [jnp.where(end, -layers * cols, 0) for end in (here == 0, here == count - 1)]
    column = (iota((1, cols), 1) >> 2) * cols + jnp.where(j < 2, j + low, cols - 4 + j + high)
    pick = jnp.where(k == column, 1.0, 0.0).astype(BF16)
    x = jnp.concatenate([x_ref[d] for d in range(layers)], axis=1)
    cols_ref[...] = jnp.dot(x, pick, preferred_element_type=F32).astype(BF16)


def slopes_kernel(x_ref, table_ref, side_ref, gc_ref, gr_ref, tabs_ref, far_ref):
    layers, rows, cols = x_ref.shape
    far_ref[...] = jnp.broadcast_to(side_ref[...], far_ref.shape)
    table = table_ref[...].astype(F32) * UNIT
    for p, (high, low) in enumerate([(0, 1), (3, 2)]):
        pair = table[high : high + 1] * PAIR + (table[low : low + 1] - MIDDLE)
        for h in range(2):
            tabs_ref[p, h] = jnp.broadcast_to(pair[:, h * HALF : (h + 1) * HALF], (8, HALF))
    inner = stencil(iota((cols, cols), 0) - iota((cols, cols), 1))
    none = jnp.zeros_like(inner)
    across = stencil(iota((rows, rows), 1) - iota((rows, rows), 0))
    along = jnp.concatenate(
        [jnp.concatenate([inner, none], axis=1), jnp.concatenate([none, inner], axis=1)], axis=0
    )
    for d in range(0, layers, 2):
        x = jnp.concatenate([x_ref[d], x_ref[d + 1]], axis=1)
        gc = jnp.dot(x, along, preferred_element_type=F32)
        gr = jnp.dot(across, x, preferred_element_type=F32)
        for i in range(2):
            gc_ref[d + i] = gc[:, i * cols : (i + 1) * cols]
            gr_ref[d + i] = gr[:, i * cols : (i + 1) * cols]


def outer_slopes(left_ref, right_ref, ge_ref):
    layers, rows, cols = ge_ref.shape
    lane = iota((rows, cols), 1)
    halo = jnp.where((lane & 2) == 0, right_ref[...], left_ref[...])
    k, c = iota((cols, cols), 0), iota((cols, cols), 1)
    j = k & 3
    outer = stencil(jnp.where(j < 2, cols + j, j - 4) - c)
    none = jnp.zeros_like(outer)
    for d in range(0, layers, 2):
        edge = jnp.concatenate([jnp.where((k >> 2) == d + i, outer, none) for i in range(2)], axis=1)
        ge = jnp.dot(halo, edge, preferred_element_type=F32)
        for i in range(2):
            ge_ref[d + i] = ge[:, i * cols : (i + 1) * cols]


def brick_kernel(depth_total, x_ref, before_ref, after_ref, left_ref, right_ref, bins_hbm, gc_ref, gr_ref, tabs_ref, far_ref, out_ref, ge_ref, bins_ref, sem):
    layers, rows, cols = x_ref.shape
    fetch = pltpu.make_async_copy(bins_hbm, bins_ref, sem)
    fetch.start()
    outer_slopes(left_ref, right_ref, ge_ref)
    tabs = [[tabs_ref[p, h] for h in range(2)] for p in range(2)]
    step = OPTICAL / depth_total
    far_side = far_ref[...] != 0
    slope = jnp.where(far_side, 1.0, -1.0) * (step / math.log(2.0) / (PAIR * UNIT))
    low, unit = colour_code(layers, depth_total)
    lx, ly, lz = LIGHT_DIRECTION
    gain = DIFFUSE * lz
    scales = [math.log(gain / (PAIR * UNIT)), math.log(gain / UNIT), math.log(gain / UNIT)]

    def layer(d, at):
        if d < 2:
            return before_ref[d, at]
        if d >= layers + 2:
            return after_ref[d - layers - 2, at]
        return x_ref[d - 2, at]

    def split(pair):
        high = (pair + ROUND) - ROUND
        return high, pair - high

    def block(b, carry):
        for g in range(GROUP):
            base = b * GROUP + g
            at = pl.ds(pl.multiple_of(base * 16, 16), 16)
            f = [layer(d, at).astype(F32) for d in range(layers + 4)]
            for h in range(2):
                at8 = pl.ds(pl.multiple_of(base * 16 + h * 8, 8), 8)
                rows8 = slice(h * 8, h * 8 + 8)
                zero = jnp.zeros((8, cols), F32)
                red, green, blue, whole, total = zero, zero, zero, zero, zero
                seen = jnp.ones((8, cols), F32)
                for d in range(layers):
                    gd = 8.0 * (f[d + 3][rows8] - f[d + 1][rows8]) - (f[d + 4][rows8] - f[d][rows8])
                    gc, gr = gc_ref[d, at8] + ge_ref[d, at8], gr_ref[d, at8]
                    light = (lx / lz) * gc + (ly / lz) * gr + gd
                    norm = lax.rsqrt(gc * gc + gr * gr + (gd * gd + 144.0))
                    shade = AMBIENT / gain + jnp.abs(light) * norm
                    index = bins_ref[d, at8]
                    upper = index >= HALF
                    index = index & (HALF - 1)
                    (r, gn), (ext, bl) = [split(jnp.where(upper, lanes(t[1], index), lanes(t[0], index))) for t in tabs]
                    total = total + ext
                    now = jnp.exp2(total * slope)
                    weight = (now - seen) * shade
                    seen = now
                    red, green, blue = red + r * weight, green + gn * weight, blue + bl * weight
                    whole = whole + weight
                shift = jnp.where(far_side, total * (-step / (PAIR * UNIT)), 0.0) - low
                code = [
                    jnp.clip((jnp.log(jnp.abs(v)) + (shift + scale)) * (1.0 / unit) + 0.5, 0.0, CODES).astype(I32)
                    for v, scale in zip((red, green + MIDDLE * whole, blue + MIDDLE * whole), scales)
                ]
                count = (total * (1.0 / PAIR) + 0.5).astype(I32)
                at_out = base * 2 + h
                out_ref[at_out, 0:8, :] = code[0] + (code[1] << 16)
                out_ref[at_out, 8:16, :] = code[2] + (count << 16)
        return carry

    fetch.wait()
    lax.fori_loop(0, rows // (16 * GROUP), block, 0)


def merge_kernel(layers, depth_total, in_ref, side_ref, out_ref):
    parts, _, cols = in_ref.shape
    step = OPTICAL / depth_total / UNIT
    low, unit = colour_code(layers, depth_total)
    far_side = jnp.broadcast_to(side_ref[...], (8, cols)) != 0
    counts = [lax.shift_right_logical(in_ref[p, 8:16, :], 16) for p in range(parts)]
    total = counts[0]
    for v in counts[1:]:
        total = total + v
    ahead = jnp.where(far_side, total, 0)
    colour = [jnp.zeros((8, cols), F32)] * 3
    for p in range(parts):
        first, second = in_ref[p, 0:8, :], in_ref[p, 8:16, :]
        codes = [first & 0xFFFF, lax.shift_right_logical(first, 16), second & 0xFFFF]
        behind = ahead - counts[p]
        shift = jnp.where(far_side, behind, ahead).astype(F32) * -step + low
        colour = [colour[i] + jnp.exp(codes[i].astype(F32) * unit + shift) for i in range(3)]
        ahead = jnp.where(far_side, behind, ahead + counts[p])
    for i in range(3):
        out_ref[i] = colour[i]
    out_ref[3] = 1.0 - jnp.exp(total.astype(F32) * -step)


def shift(x, axis, up):
    count = lax.axis_size(axis)
    pairs = [(i, (i + 1) % count) for i in range(count)]
    return lax.ppermute(x, axis, pairs if up else [(b, a) for a, b in pairs])


def local(kernel, name, outs, *args, scratch=(), limit=16, stay=()):
    vmem, there = pl.BlockSpec(memory_space=pltpu.VMEM), pl.BlockSpec(memory_space=pltpu.HBM)
    return pl.pallas_call(
        kernel,
        out_shape=[pltpu.VMEM(s, d) for s, d in outs],
        in_specs=[there if i in stay else vmem for i in range(len(args))],
        out_specs=[vmem] * len(outs),
        scratch_shapes=list(scratch),
        compiler_params=pltpu.CompilerParams(vmem_limit_bytes=limit << 20),
        name=name,
    )(*[pltpu.with_memory_space_constraint(a, pltpu.HBM if i in stay else pltpu.VMEM) for i, a in enumerate(args)])


def on_device(density, bin_index, transfer, view_side):
    layers, rows, cols = density.shape
    count = lax.axis_size("depth")
    depth_total = layers * count
    block_rows = rows // count
    brick_f32 = ((layers, rows, cols), F32)
    first, last = local(
        faces_kernel, "faces", [((2, rows, cols), BF16)] * 2, density, scratch=[pltpu.SemaphoreType.DMA((2,))], stay=(0,)
    )
    before = shift(last, "depth", True)
    after = shift(first, "depth", False)
    (columns,) = local(columns_kernel, "columns", [((rows, cols), BF16)], density)
    left = shift(columns, "screen", True)
    right = shift(columns, "screen", False)
    side = view_side.reshape(1, cols)
    slopes = local(
        slopes_kernel,
        "slopes",
        [brick_f32] * 2 + [((2, 2, 8, HALF), F32), ((8, cols), I32)],
        *(density, transfer, side),
    )
    (tiles,) = local(
        lambda *refs: brick_kernel(depth_total, *refs),
        "brick",
        [((count, 2 * block_rows, cols), I32)],
        *(density, before, after, left, right, bin_index, *slopes),
        scratch=[pltpu.VMEM(*brick_f32), pltpu.VMEM((layers, rows, cols), I32), pltpu.SemaphoreType.DMA(())],
        stay=(5,),
    )
    arrived = lax.all_to_all(tiles, "depth", split_axis=0, concat_axis=0, tiled=True)
    return pl.pallas_call(
        lambda *refs: merge_kernel(layers, depth_total, *refs),
        out_shape=jax.ShapeDtypeStruct((4, block_rows, cols), F32),
        in_specs=[pl.BlockSpec(memory_space=pltpu.VMEM)] * 2,
        compiler_params=pltpu.CompilerParams(vmem_limit_bytes=16 << 20),
        name="merge",
    )(*[pltpu.with_memory_space_constraint(a, pltpu.VMEM) for a in (arrived, side)])


def solution(mesh):
    placed = (P("depth", None, "screen"), P("depth", None, "screen"), P(), P("screen"))
    return jax.shard_map(
        on_device, mesh=mesh, in_specs=placed, out_specs=P(None, "depth", "screen"), check_vma=False
    )
```

```python
import jax
import jax.numpy as jnp
from jax import lax
from jax.experimental import pallas as pl
from jax.experimental.pallas import tpu as pltpu
from jax.sharding import PartitionSpec as P
import math

LIGHT_DIRECTION = (0.36, 0.48, 0.8)
AMBIENT = 0.3
DIFFUSE = 0.7
OPTICAL = 4.0
LEAST = 0.049804688
UNIT = 4096.0
CODES = 65535.0
HALF = 128
PAIR = 4096.0
MIDDLE = 2150.0
ROUND = 1.5 * 2.0**23 * PAIR

F32, BF16, I32 = jnp.float32, jnp.bfloat16, jnp.int32


def stencil(offset):
    one = jnp.where(offset > 0, 8.0, -8.0)
    two = jnp.where(offset > 0, -1.0, 1.0)
    far = jnp.abs(offset)
    return jnp.where(far == 1, one, jnp.where(far == 2, two, 0.0)).astype(BF16)


def iota(shape, dim):
    return lax.broadcasted_iota(I32, shape, dim)


def colour_code(layers, depth_total):
    step = OPTICAL / depth_total
    low = LEAST * AMBIENT * -math.expm1(-layers * LEAST * step) * 0.999
    high = -math.expm1(-layers * step) * 1.001
    return math.log(low), math.log(high / low) / CODES


def lanes(table, index):
    numbers = lax.GatherDimensionNumbers((), (1,), (1,), (0,), (0,))
    return lax.gather(
        table, index[..., None], numbers, (1, 1), mode=lax.GatherScatterMode.PROMISE_IN_BOUNDS
    )


def faces_kernel(x_hbm, first_ref, second_ref, sems):
    layers = x_hbm.shape[0]
    here, count = lax.axis_index("depth"), lax.axis_size("depth")
    odd = here & 1
    starts = [(1 - odd) * (layers - 2), odd * (layers - 2)]
    copies = [
        pltpu.make_async_copy(x_hbm.at[pl.ds(start, 2)], ref, sems.at[i])
        for i, (start, ref) in enumerate(zip(starts, (first_ref, second_ref)))
    ]
    for copy in copies:
        copy.start()
    for copy in copies:
        copy.wait()

    @pl.when((here == 0) | (here == count - 1))
    def _():
        second_ref[...] = jnp.zeros_like(second_ref)


def columns_kernel(x_ref, cols_ref):
    layers, _, cols = x_ref.shape
    k = iota((layers * cols, cols), 0)
    j = iota((1, cols), 1) & 3
    column = (iota((1, cols), 1) >> 2) * cols + jnp.where(j < 2, j, cols - 4 + j)
    pick = jnp.where(k == column, 1.0, 0.0).astype(BF16)
    x = jnp.concatenate([x_ref[d] for d in range(layers)], axis=1)
    cols_ref[...] = jnp.dot(x, pick, preferred_element_type=F32).astype(BF16)


def slopes_kernel(x_ref, table_ref, side_ref, gc_ref, gr_ref, tabs_ref, far_ref):
    layers, rows, cols = x_ref.shape
    far_ref[...] = jnp.broadcast_to(side_ref[...], far_ref.shape)
    table = table_ref[...].astype(F32) * UNIT
    for p, (high, low) in enumerate([(0, 1), (3, 2)]):
        pair = table[high : high + 1] * PAIR + (table[low : low + 1] - MIDDLE)
        for h in range(2):
            tabs_ref[p, h] = jnp.broadcast_to(pair[:, h * HALF : (h + 1) * HALF], (8, HALF))
    inner = stencil(iota((cols, cols), 0) - iota((cols, cols), 1))
    none = jnp.zeros_like(inner)
    across = stencil(iota((rows, rows), 1) - iota((rows, rows), 0))
    along = jnp.concatenate(
        [jnp.concatenate([inner, none], axis=1), jnp.concatenate([none, inner], axis=1)], axis=0
    )
    for d in range(0, layers, 2):
        x = jnp.concatenate([x_ref[d], x_ref[d + 1]], axis=1)
        gc = jnp.dot(x, along, preferred_element_type=F32)
        gr = jnp.dot(across, x, preferred_element_type=F32)
        for i in range(2):
            gc_ref[d + i] = gc[:, i * cols : (i + 1) * cols]
            gr_ref[d + i] = gr[:, i * cols : (i + 1) * cols]


def outer_slopes(first_ref, second_ref, ge_ref):
    layers, rows, cols = ge_ref.shape
    here, count = lax.axis_index("screen"), lax.axis_size("screen")
    outermost = jnp.where((here == 0) | (here == count - 1), 2, 0)
    source = (((iota((rows, cols), 1) >> 1) & 1) ^ (here & 1)) + outermost
    first, second = first_ref[...], second_ref[...]
    halo = jnp.where((source & 1) == 0, first, jnp.where(source == 1, second, jnp.zeros_like(second)))
    k, c = iota((cols, cols), 0), iota((cols, cols), 1)
    j = k & 3
    outer = stencil(jnp.where(j < 2, cols + j, j - 4) - c)
    none = jnp.zeros_like(outer)
    for d in range(0, layers, 2):
        edge = jnp.concatenate([jnp.where((k >> 2) == d + i, outer, none) for i in range(2)], axis=1)
        ge = jnp.dot(halo, edge, preferred_element_type=F32)
        for i in range(2):
            ge_ref[d + i] = ge[:, i * cols : (i + 1) * cols]


def brick_kernel(depth_total, x_ref, depth0_ref, depth1_ref, screen0_ref, screen1_ref, bins_hbm, gc_ref, gr_ref, tabs_ref, far_ref, out_ref, ge_ref, bins_ref, even_ref, odd_ref, sem):
    layers, rows, cols = x_ref.shape
    fetch = pltpu.make_async_copy(bins_hbm, bins_ref, sem)
    fetch.start()
    outer_slopes(screen0_ref, screen1_ref, ge_ref)
    tabs = [[tabs_ref[p, h] for h in range(2)] for p in range(2)]
    step = OPTICAL / depth_total
    far_side = far_ref[...] != 0
    slope = jnp.where(far_side, 1.0, -1.0) * (step / math.log(2.0) / (PAIR * UNIT))
    low, unit = colour_code(layers, depth_total)
    lx, ly, lz = LIGHT_DIRECTION
    gain = DIFFUSE * lz
    scales = [math.log(gain / (PAIR * UNIT)), math.log(gain / UNIT), math.log(gain / UNIT)]
    is_odd = (lax.axis_index("depth") & 1) == 1

    def layer(d, at):
        if 2 <= d < layers + 2:
            return x_ref[d - 2, at]
        zero, one = [ref[d % (layers + 2), at] for ref in (depth0_ref, depth1_ref)]
        return jnp.where(is_odd == (d < 2), zero, one)

    def split(pair):
        high = (pair + ROUND) - ROUND
        return high, pair - high

    def rows_of(b, h):
        return pl.ds(pl.multiple_of(b * 16 + h * 8, 8), 8)

    def look_up(b, word_ref):
        for h in range(2):
            for d in range(layers):
                index = bins_ref[d, rows_of(b, h)]
                upper = index >= HALF
                index = index & (HALF - 1)
                for p, t in enumerate(tabs):
                    word_ref[p, d, h * 8 : h * 8 + 8] = jnp.where(upper, lanes(t[1], index), lanes(t[0], index))

    def render(b, word_ref):
        at = pl.ds(pl.multiple_of(b * 16, 16), 16)
        f = [layer(d, at).astype(F32) for d in range(layers + 4)]
        for h in range(2):
            at8, rows8 = rows_of(b, h), slice(h * 8, h * 8 + 8)
            zero = jnp.zeros((8, cols), F32)
            red, green, blue, whole, total = zero, zero, zero, zero, zero
            seen = jnp.ones((8, cols), F32)
            for d in range(layers):
                gd = 8.0 * (f[d + 3][rows8] - f[d + 1][rows8]) - (f[d + 4][rows8] - f[d][rows8])
                gc, gr = gc_ref[d, at8] + ge_ref[d, at8], gr_ref[d, at8]
                light = (lx / lz) * gc + (ly / lz) * gr + gd
                norm = lax.rsqrt(gc * gc + gr * gr + (gd * gd + 144.0))
                shade = AMBIENT / gain + jnp.abs(light) * norm
                (r, gn), (ext, bl) = [split(word_ref[p, d, rows8]) for p in range(2)]
                total = total + ext
                now = jnp.exp2(total * slope)
                weight = (now - seen) * shade
                seen = now
                red, green, blue = red + r * weight, green + gn * weight, blue + bl * weight
                whole = whole + weight
            shift = jnp.where(far_side, total * (-step / (PAIR * UNIT)), 0.0) - low
            code = [
                jnp.clip((jnp.log(jnp.abs(v)) + (shift + scale)) * (1.0 / unit) + 0.5, 0.0, CODES).astype(I32)
                for v, scale in zip((red, green + MIDDLE * whole, blue + MIDDLE * whole), scales)
            ]
            count = (total * (1.0 / PAIR) + 0.5).astype(I32)
            out_ref[b * 2 + h, 0:8, :] = code[0] + (code[1] << 16)
            out_ref[b * 2 + h, 8:16, :] = code[2] + (count << 16)

    blocks = rows // 16

    def two(i, carry):
        b = 2 * i
        look_up(b + 1, odd_ref)
        render(b, even_ref)
        look_up(jnp.minimum(b + 2, blocks - 1), even_ref)
        render(b + 1, odd_ref)
        return carry

    fetch.wait()
    look_up(0, even_ref)
    lax.fori_loop(0, blocks // 2, two, 0)


def merge_kernel(layers, depth_total, in_ref, side_ref, out_ref):
    parts, _, cols = in_ref.shape
    step = OPTICAL / depth_total / UNIT
    low, unit = colour_code(layers, depth_total)
    far_side = jnp.broadcast_to(side_ref[...], (8, cols)) != 0
    counts = [lax.shift_right_logical(in_ref[p, 8:16, :], 16) for p in range(parts)]
    total = counts[0]
    for v in counts[1:]:
        total = total + v
    ahead = jnp.where(far_side, total, 0)
    colour = [jnp.zeros((8, cols), F32)] * 3
    for p in range(parts):
        first, second = in_ref[p, 0:8, :], in_ref[p, 8:16, :]
        codes = [first & 0xFFFF, lax.shift_right_logical(first, 16), second & 0xFFFF]
        behind = ahead - counts[p]
        shift = jnp.where(far_side, behind, ahead).astype(F32) * -step + low
        colour = [colour[i] + jnp.exp(codes[i].astype(F32) * unit + shift) for i in range(3)]
        ahead = jnp.where(far_side, behind, ahead + counts[p])
    for i in range(3):
        out_ref[i] = colour[i]
    out_ref[3] = 1.0 - jnp.exp(total.astype(F32) * -step)


def swap(x, axis, odd):
    count = lax.axis_size(axis)
    pairs = [(i, i + 1) for i in range(odd, count - 1, 2)]
    alone = [(i, i) for i in (0, count - 1)] if odd else []
    return lax.ppermute(x, axis, pairs + [(b, a) for a, b in pairs] + alone)


def local(kernel, name, outs, *args, scratch=(), limit=16, stay=()):
    vmem, there = pl.BlockSpec(memory_space=pltpu.VMEM), pl.BlockSpec(memory_space=pltpu.HBM)
    return pl.pallas_call(
        kernel,
        out_shape=[pltpu.VMEM(s, d) for s, d in outs],
        in_specs=[there if i in stay else vmem for i in range(len(args))],
        out_specs=[vmem] * len(outs),
        scratch_shapes=list(scratch),
        compiler_params=pltpu.CompilerParams(vmem_limit_bytes=limit << 20),
        name=name,
    )(*[pltpu.with_memory_space_constraint(a, pltpu.HBM if i in stay else pltpu.VMEM) for i, a in enumerate(args)])


def on_device(density, bin_index, transfer, view_side):
    layers, rows, cols = density.shape
    count = lax.axis_size("depth")
    depth_total = layers * count
    block_rows = rows // count
    brick_f32 = ((layers, rows, cols), F32)
    faces = local(
        faces_kernel, "faces", [((2, rows, cols), BF16)] * 2, density, scratch=[pltpu.SemaphoreType.DMA((2,))], stay=(0,)
    )
    beside = [swap(faces[odd], "depth", odd) for odd in range(2)]
    (columns,) = local(columns_kernel, "columns", [((rows, cols), BF16)], density)
    beside += [swap(columns, "screen", odd) for odd in range(2)]
    side = view_side.reshape(1, cols)
    slopes = local(
        slopes_kernel,
        "slopes",
        [brick_f32] * 2 + [((2, 2, 8, HALF), F32), ((8, cols), I32)],
        *(density, transfer, side),
    )
    (tiles,) = local(
        lambda *refs: brick_kernel(depth_total, *refs),
        "brick",
        [((count, 2 * block_rows, cols), I32)],
        *(density, *beside, bin_index, *slopes),
        scratch=[
            pltpu.VMEM(*brick_f32),
            pltpu.VMEM((layers, rows, cols), I32),
            pltpu.VMEM((2, layers, 16, cols), F32),
            pltpu.VMEM((2, layers, 16, cols), F32),
            pltpu.SemaphoreType.DMA(()),
        ],
        stay=(5,),
    )
    arrived = lax.all_to_all(tiles, "depth", split_axis=0, concat_axis=0, tiled=True)
    return pl.pallas_call(
        lambda *refs: merge_kernel(layers, depth_total, *refs),
        out_shape=jax.ShapeDtypeStruct((4, block_rows, cols), F32),
        in_specs=[pl.BlockSpec(memory_space=pltpu.VMEM)] * 2,
        compiler_params=pltpu.CompilerParams(vmem_limit_bytes=16 << 20),
        name="merge",
    )(*[pltpu.with_memory_space_constraint(a, pltpu.VMEM) for a in (arrived, side)])


def solution(mesh):
    placed = (P("depth", None, "screen"), P("depth", None, "screen"), P(), P("screen"))
    return jax.shard_map(
        on_device, mesh=mesh, in_specs=placed, out_specs=P(None, "depth", "screen"), check_vma=False
    )
```

```python
import jax
import jax.numpy as jnp
from jax import lax
from jax.experimental import pallas as pl
from jax.experimental.pallas import tpu as pltpu
from jax.sharding import PartitionSpec as P
import math

LIGHT_DIRECTION = (0.36, 0.48, 0.8)
AMBIENT = 0.3
DIFFUSE = 0.7
OPTICAL = 4.0
LEAST = 0.049804688
UNIT = 4096.0
CODES = 65535.0
HALF = 128
PAIR = 4096.0
MIDDLE = 2150.0
ROUND = 1.5 * 2.0**23 * PAIR

F32, BF16, I32 = jnp.float32, jnp.bfloat16, jnp.int32


def stencil(offset):
    one = jnp.where(offset > 0, 8.0, -8.0)
    two = jnp.where(offset > 0, -1.0, 1.0)
    far = jnp.abs(offset)
    return jnp.where(far == 1, one, jnp.where(far == 2, two, 0.0)).astype(BF16)


def iota(shape, dim):
    return lax.broadcasted_iota(I32, shape, dim)


def colour_code(layers, depth_total):
    step = OPTICAL / depth_total
    low = LEAST * AMBIENT * -math.expm1(-layers * LEAST * step) * 0.999
    high = -math.expm1(-layers * step) * 1.001
    return math.log(low), math.log(high / low) / CODES


def lanes(table, index):
    numbers = lax.GatherDimensionNumbers((), (1,), (1,), (0,), (0,))
    return lax.gather(
        table, index[..., None], numbers, (1, 1), mode=lax.GatherScatterMode.PROMISE_IN_BOUNDS
    )


def along_depth(two_before, before, after, two_after):
    return 8.0 * (after - before) - (two_after - two_before)


def faces_kernel(x_hbm, first_ref, second_ref, sems):
    layers = x_hbm.shape[0]
    here, count = lax.axis_index("depth"), lax.axis_size("depth")
    odd = here & 1
    starts = [(1 - odd) * (layers - 2), odd * (layers - 2)]
    quarter = x_hbm.shape[1] // 4
    copies = [
        pltpu.make_async_copy(
            x_hbm.at[pl.ds(start, 2), pl.ds(q * quarter, quarter)], ref.at[:, pl.ds(q * quarter, quarter)], sems.at[i * 4 + q]
        )
        for i, (start, ref) in enumerate(zip(starts, (first_ref, second_ref)))
        for q in range(4)
    ]
    for copy in copies:
        copy.start()
    for copy in copies:
        copy.wait()

    @pl.when((here == 0) | (here == count - 1))
    def _():
        second_ref[...] = jnp.zeros_like(second_ref)


def columns_kernel(x_ref, cols_ref):
    layers, _, cols = x_ref.shape
    k = iota((layers * cols, cols), 0)
    j = iota((1, cols), 1) & 3
    column = (iota((1, cols), 1) >> 2) * cols + jnp.where(j < 2, j, cols - 4 + j)
    pick = jnp.where(k == column, 1.0, 0.0).astype(BF16)
    x = jnp.concatenate([x_ref[d] for d in range(layers)], axis=1)
    cols_ref[...] = jnp.dot(x, pick, preferred_element_type=F32).astype(BF16)


def slopes_kernel(x_ref, table_hbm, side_hbm, gc_ref, light_ref, square_ref, edge_ref, tabs_ref, far_ref, table_ref, side_ref, sems):
    layers, rows, cols = x_ref.shape
    copies = [
        pltpu.make_async_copy(hbm, ref, sems.at[i])
        for i, (hbm, ref) in enumerate([(table_hbm, table_ref), (side_hbm, side_ref)])
    ]
    for copy in copies:
        copy.start()
    k, c = iota((cols, cols), 0), iota((cols, cols), 1)
    inner = stencil(k - c)
    none = jnp.zeros_like(inner)
    across = stencil(iota((rows, rows), 1) - iota((rows, rows), 0))
    along = jnp.concatenate(
        [jnp.concatenate([inner, none], axis=1), jnp.concatenate([none, inner], axis=1)], axis=0
    )
    ly, lz = LIGHT_DIRECTION[1:]
    for d in range(0, layers, 2):
        x = jnp.concatenate([x_ref[d], x_ref[d + 1]], axis=1)
        gc = jnp.dot(x, along, preferred_element_type=F32)
        gr = jnp.dot(across, x, preferred_element_type=F32)
        for e in range(d, d + 2):
            at = slice((e - d) * cols, (e - d + 1) * cols)
            gc_ref[e] = gc[:, at]
            light = (ly / lz) * gr[:, at]
            square = gr[:, at] * gr[:, at] + 144.0
            if 2 <= e < layers - 2:
                gd = along_depth(*[x_ref[e + i].astype(F32) for i in (-2, -1, 1, 2)])
                light = light + gd
                square = square + gd * gd
            light_ref[e] = light
            square_ref[e] = square
    j = k & 3
    outer = stencil(jnp.where(j < 2, cols + j, j - 4) - c)
    for d in range(layers):
        edge_ref[d // 2, :, (d % 2) * cols : (d % 2 + 1) * cols] = jnp.where((k >> 2) == d, outer, none)
    for copy in copies:
        copy.wait()
    far_ref[...] = jnp.broadcast_to(side_ref[...], far_ref.shape)
    table = table_ref[...].astype(F32) * UNIT
    for p, (high, low) in enumerate([(0, 1), (3, 2)]):
        pair = table[high : high + 1] * PAIR + (table[low : low + 1] - MIDDLE)
        for h in range(2):
            tabs_ref[p, h] = jnp.broadcast_to(pair[:, h * HALF : (h + 1) * HALF], (8, HALF))


def outer_slopes(first_ref, second_ref, edge_ref, ge_ref):
    layers, rows, cols = ge_ref.shape
    here, count = lax.axis_index("screen"), lax.axis_size("screen")
    outermost = jnp.where((here == 0) | (here == count - 1), 2, 0)
    source = (((iota((rows, cols), 1) >> 1) & 1) ^ (here & 1)) + outermost
    first, second = first_ref[...], second_ref[...]
    halo = jnp.where((source & 1) == 0, first, jnp.where(source == 1, second, jnp.zeros_like(second)))
    for d in range(0, layers, 2):
        ge = jnp.dot(halo, edge_ref[d // 2], preferred_element_type=F32)
        for i in range(2):
            ge_ref[d + i] = ge[:, i * cols : (i + 1) * cols]


def brick_kernel(depth_total, x_ref, depth0_ref, depth1_ref, screen0_ref, screen1_ref, bins_ref, gc_ref, light_ref, square_ref, edge_ref, tabs_ref, far_ref, out_ref, ge_ref, even_ref, odd_ref):
    layers, rows, cols = x_ref.shape
    outer_slopes(screen0_ref, screen1_ref, edge_ref, ge_ref)
    tabs = [[tabs_ref[p, h] for h in range(2)] for p in range(2)]
    step = OPTICAL / depth_total
    far_side = far_ref[...] != 0
    slope = jnp.where(far_side, 1.0, -1.0) * (step / math.log(2.0) / (PAIR * UNIT))
    low, unit = colour_code(layers, depth_total)
    lx, _, lz = LIGHT_DIRECTION
    gain = DIFFUSE * lz
    scales = [(math.log(gain / scale) - low) / unit + 0.5 for scale in (PAIR * UNIT, UNIT, UNIT)]
    is_odd = (lax.axis_index("depth") & 1) == 1

    def layer(d, at):
        if 2 <= d < layers + 2:
            return x_ref[d - 2, at]
        zero, one = [ref[d % (layers + 2), at] for ref in (depth0_ref, depth1_ref)]
        return jnp.where(is_odd == (d < 2), zero, one)

    def split(pair):
        high = (pair + ROUND) - ROUND
        return high, pair - high

    def rows_of(b, h):
        return pl.ds(pl.multiple_of(b * 16 + h * 8, 8), 8)

    def look_up(b, word_ref):
        for h in range(2):
            for d in range(layers):
                index = bins_ref[d, rows_of(b, h)]
                upper = index >= HALF
                index = index & (HALF - 1)
                for p, t in enumerate(tabs):
                    word_ref[p, d, h * 8 : h * 8 + 8] = jnp.where(upper, lanes(t[1], index), lanes(t[0], index))

    def render(b, word_ref):
        at = pl.ds(pl.multiple_of(b * 16, 16), 16)
        f = [layer(d, at).astype(F32) for d in range(layers + 4)]
        for h in range(2):
            at8, rows8 = rows_of(b, h), slice(h * 8, h * 8 + 8)
            zero = jnp.zeros((8, cols), F32)
            red, green, blue, whole, total = zero, zero, zero, zero, zero
            seen = jnp.ones((8, cols), F32)
            for d in range(layers):
                gc = gc_ref[d, at8] + ge_ref[d, at8]
                light = (lx / lz) * gc + light_ref[d, at8]
                square = gc * gc + square_ref[d, at8]
                if not 2 <= d < layers - 2:
                    gd = along_depth(*[f[d + i][rows8] for i in (0, 1, 3, 4)])
                    light = light + gd
                    square = square + gd * gd
                shade = AMBIENT / gain + jnp.abs(light) * lax.rsqrt(square)
                (r, gn), (ext, bl) = [split(word_ref[p, d, rows8]) for p in range(2)]
                total = total + ext
                now = jnp.exp2(total * slope)
                weight = (now - seen) * shade
                seen = now
                red, green, blue = red + r * weight, green + gn * weight, blue + bl * weight
                whole = whole + weight
            shift = jnp.where(far_side, total * (-step / (PAIR * UNIT * unit)), 0.0)
            code = [
                (jnp.log(jnp.abs(v)) * (1.0 / unit) + (shift + scale)).astype(I32)
                for v, scale in zip((red, green + MIDDLE * whole, blue + MIDDLE * whole), scales)
            ]
            count = (total * (1.0 / PAIR) + 0.5).astype(I32)
            out_ref[b * 2 + h, 0:8, :] = code[0] + (code[1] << 16)
            out_ref[b * 2 + h, 8:16, :] = code[2] + (count << 16)

    blocks = rows // 16

    def two(i, carry):
        b = 2 * i
        look_up(b + 1, odd_ref)
        render(b, even_ref)
        look_up(jnp.minimum(b + 2, blocks - 1), even_ref)
        render(b + 1, odd_ref)
        return carry

    look_up(0, even_ref)
    lax.fori_loop(0, blocks // 2, two, 0)


def merge_kernel(layers, depth_total, in_ref, far_ref, out_ref):
    parts, _, cols = in_ref.shape
    step = OPTICAL / depth_total / UNIT
    low, unit = colour_code(layers, depth_total)
    far_side = far_ref[...] != 0
    counts = [lax.shift_right_logical(in_ref[p, 8:16, :], 16) for p in range(parts)]
    total = counts[0]
    for v in counts[1:]:
        total = total + v
    ahead = jnp.where(far_side, total, 0)
    colour = [jnp.zeros((8, cols), F32)] * 3
    for p in range(parts):
        first, second = in_ref[p, 0:8, :], in_ref[p, 8:16, :]
        codes = [first & 0xFFFF, lax.shift_right_logical(first, 16), second & 0xFFFF]
        behind = ahead - counts[p]
        shift = jnp.where(far_side, behind, ahead).astype(F32) * -step + low
        colour = [colour[i] + jnp.exp(codes[i].astype(F32) * unit + shift) for i in range(3)]
        ahead = jnp.where(far_side, behind, ahead + counts[p])
    for i in range(3):
        out_ref[i] = colour[i]
    out_ref[3] = 1.0 - jnp.exp(total.astype(F32) * -step)


def swap(x, axis, odd):
    count = lax.axis_size(axis)
    pairs = [(i, i + 1) for i in range(odd, count - 1, 2)]
    alone = [(i, i) for i in (0, count - 1)] if odd else []
    return lax.ppermute(x, axis, pairs + [(b, a) for a, b in pairs] + alone)


def local(kernel, name, outs, *args, scratch=(), limit=16, stay=()):
    vmem, there = pl.BlockSpec(memory_space=pltpu.VMEM), pl.BlockSpec(memory_space=pltpu.HBM)
    return pl.pallas_call(
        kernel,
        out_shape=[pltpu.VMEM(s, d) for s, d in outs],
        in_specs=[there if i in stay else vmem for i in range(len(args))],
        out_specs=[vmem] * len(outs),
        scratch_shapes=list(scratch),
        compiler_params=pltpu.CompilerParams(vmem_limit_bytes=limit << 20),
        name=name,
    )(*[pltpu.with_memory_space_constraint(a, pltpu.HBM if i in stay else pltpu.VMEM) for i, a in enumerate(args)])


def on_device(density, bin_index, transfer, view_side):
    layers, rows, cols = density.shape
    count = lax.axis_size("depth")
    depth_total = layers * count
    block_rows = rows // count
    brick_f32 = ((layers, rows, cols), F32)
    faces = local(
        faces_kernel, "faces", [((2, rows, cols), BF16)] * 2, density, scratch=[pltpu.SemaphoreType.DMA((8,))], stay=(0,)
    )
    beside = [swap(faces[odd], "depth", odd) for odd in range(2)]
    (columns,) = local(columns_kernel, "columns", [((rows, cols), BF16)], density)
    beside += [swap(columns, "screen", odd) for odd in range(2)]
    side = view_side.reshape(1, cols)
    slopes = local(
        slopes_kernel,
        "slopes",
        [brick_f32] * 3
        + [((layers // 2, cols, 2 * cols), BF16), ((2, 2, 8, HALF), F32), ((8, cols), I32)],
        *(density, transfer, side),
        scratch=[pltpu.VMEM(transfer.shape, BF16), pltpu.VMEM(side.shape, I32), pltpu.SemaphoreType.DMA((2,))],
        stay=(1, 2),
    )
    (tiles,) = local(
        lambda *refs: brick_kernel(depth_total, *refs),
        "brick",
        [((count, 2 * block_rows, cols), I32)],
        *(density, *beside, bin_index, *slopes),
        scratch=[
            pltpu.VMEM(*brick_f32),
            pltpu.VMEM((2, layers, 16, cols), F32),
            pltpu.VMEM((2, layers, 16, cols), F32),
        ],
    )
    arrived = lax.all_to_all(tiles, "depth", split_axis=0, concat_axis=0, tiled=True)
    return pl.pallas_call(
        lambda *refs: merge_kernel(layers, depth_total, *refs),
        out_shape=jax.ShapeDtypeStruct((4, block_rows, cols), F32),
        in_specs=[pl.BlockSpec(memory_space=pltpu.VMEM)] * 2,
        compiler_params=pltpu.CompilerParams(vmem_limit_bytes=16 << 20),
        name="merge",
    )(*[pltpu.with_memory_space_constraint(a, pltpu.VMEM) for a in (arrived, slopes[-1])])


def solution(mesh):
    placed = (P("depth", None, "screen"), P("depth", None, "screen"), P(), P("screen"))
    return jax.shard_map(
        on_device, mesh=mesh, in_specs=placed, out_specs=P(None, "depth", "screen"), check_vma=False
    )
```

```python
import jax
import jax.numpy as jnp
from jax import lax
from jax.experimental import pallas as pl
from jax.experimental.pallas import tpu as pltpu
from jax.sharding import PartitionSpec as P
import math

LIGHT_DIRECTION = (0.36, 0.48, 0.8)
AMBIENT = 0.3
DIFFUSE = 0.7
OPTICAL = 4.0
LEAST = 0.049804688
UNIT = 4096.0
CODES = 65535.0
HALF = 128
PAIR = 4096.0
MIDDLE = 2150.0
ROUND = 1.5 * 2.0**23 * PAIR

F32, BF16, I32 = jnp.float32, jnp.bfloat16, jnp.int32


def stencil(offset):
    one = jnp.where(offset > 0, 8.0, -8.0)
    two = jnp.where(offset > 0, -1.0, 1.0)
    far = jnp.abs(offset)
    return jnp.where(far == 1, one, jnp.where(far == 2, two, 0.0)).astype(BF16)


def iota(shape, dim):
    return lax.broadcasted_iota(I32, shape, dim)


def colour_code(layers, depth_total):
    step = OPTICAL / depth_total
    low = LEAST * AMBIENT * -math.expm1(-layers * LEAST * step) * 0.999
    high = -math.expm1(-layers * step) * 1.001
    return math.log(low), math.log(high / low) / CODES


def lanes(table, index):
    numbers = lax.GatherDimensionNumbers((), (1,), (1,), (0,), (0,))
    return lax.gather(
        table, index[..., None], numbers, (1, 1), mode=lax.GatherScatterMode.PROMISE_IN_BOUNDS
    )


def along_depth(two_before, before, after, two_after):
    return 8.0 * (after - before) - (two_after - two_before)


def faces_kernel(x_hbm, first_ref, second_ref, sems):
    layers = x_hbm.shape[0]
    here, count = lax.axis_index("depth"), lax.axis_size("depth")
    odd = here & 1
    starts = [(1 - odd) * (layers - 2), odd * (layers - 2)]
    quarter = x_hbm.shape[1] // 4
    copies = [
        pltpu.make_async_copy(
            x_hbm.at[pl.ds(start, 2), pl.ds(q * quarter, quarter)], ref.at[:, pl.ds(q * quarter, quarter)], sems.at[i * 4 + q]
        )
        for i, (start, ref) in enumerate(zip(starts, (first_ref, second_ref)))
        for q in range(4)
    ]
    for copy in copies:
        copy.start()
    for copy in copies:
        copy.wait()

    @pl.when((here == 0) | (here == count - 1))
    def _():
        second_ref[...] = jnp.zeros_like(second_ref)


def columns_kernel(x_ref, cols_ref):
    layers, _, cols = x_ref.shape
    k = iota((layers * cols, cols), 0)
    j = iota((1, cols), 1) & 3
    column = (iota((1, cols), 1) >> 2) * cols + jnp.where(j < 2, j, cols - 4 + j)
    pick = jnp.where(k == column, 1.0, 0.0).astype(BF16)
    x = jnp.concatenate([x_ref[d] for d in range(layers)], axis=1)
    cols_ref[...] = jnp.dot(x, pick, preferred_element_type=F32).astype(BF16)


def slopes_kernel(x_ref, table_hbm, side_hbm, gc_ref, light_ref, square_ref, edge_ref, tabs_ref, far_ref, table_ref, side_ref, sems):
    layers, rows, cols = x_ref.shape
    copies = [
        pltpu.make_async_copy(hbm, ref, sems.at[i])
        for i, (hbm, ref) in enumerate([(table_hbm, table_ref), (side_hbm, side_ref)])
    ]
    for copy in copies:
        copy.start()
    k, c = iota((cols, cols), 0), iota((cols, cols), 1)
    inner = stencil(k - c)
    none = jnp.zeros_like(inner)
    across = stencil(iota((rows, rows), 1) - iota((rows, rows), 0))
    along = jnp.concatenate(
        [jnp.concatenate([inner, none], axis=1), jnp.concatenate([none, inner], axis=1)], axis=0
    )
    ly, lz = LIGHT_DIRECTION[1:]
    for d in range(0, layers, 2):
        x = jnp.concatenate([x_ref[d], x_ref[d + 1]], axis=1)
        gc = jnp.dot(x, along, preferred_element_type=F32)
        gr = jnp.dot(across, x, preferred_element_type=F32)
        for e in range(d, d + 2):
            at = slice((e - d) * cols, (e - d + 1) * cols)
            gc_ref[e] = gc[:, at]
            light = (ly / lz) * gr[:, at]
            square = gr[:, at] * gr[:, at] + 144.0
            if 2 <= e < layers - 2:
                gd = along_depth(*[x_ref[e + i].astype(F32) for i in (-2, -1, 1, 2)])
                light = light + gd
                square = square + gd * gd
            light_ref[e] = light
            square_ref[e] = square
    j = k & 3
    outer = stencil(jnp.where(j < 2, cols + j, j - 4) - c)
    for d in range(layers):
        edge_ref[d // 2, :, (d % 2) * cols : (d % 2 + 1) * cols] = jnp.where((k >> 2) == d, outer, none)
    for copy in copies:
        copy.wait()
    far_ref[...] = jnp.broadcast_to(side_ref[...], far_ref.shape)
    table = table_ref[...].astype(F32) * UNIT
    for p, (high, low) in enumerate([(0, 1), (3, 2)]):
        pair = table[high : high + 1] * PAIR + (table[low : low + 1] - MIDDLE)
        for h in range(2):
            tabs_ref[p, h] = jnp.broadcast_to(pair[:, h * HALF : (h + 1) * HALF], (8, HALF))


def outer_slopes(first_ref, second_ref, edge_ref, ge_ref):
    layers, rows, cols = ge_ref.shape
    here, count = lax.axis_index("screen"), lax.axis_size("screen")
    outermost = jnp.where((here == 0) | (here == count - 1), 2, 0)
    source = (((iota((rows, cols), 1) >> 1) & 1) ^ (here & 1)) + outermost
    first, second = first_ref[...], second_ref[...]
    halo = jnp.where((source & 1) == 0, first, jnp.where(source == 1, second, jnp.zeros_like(second)))
    for d in range(0, layers, 2):
        ge = jnp.dot(halo, edge_ref[d // 2], preferred_element_type=F32)
        for i in range(2):
            ge_ref[d + i] = ge[:, i * cols : (i + 1) * cols]


def brick_kernel(depth_total, x_ref, depth0_ref, depth1_ref, screen0_ref, screen1_ref, bins_ref, gc_ref, light_ref, square_ref, edge_ref, tabs_ref, far_ref, out_ref, ge_ref, even_ref, odd_ref):
    layers, rows, cols = x_ref.shape
    outer_slopes(screen0_ref, screen1_ref, edge_ref, ge_ref)
    tabs = [[tabs_ref[p, h] for h in range(2)] for p in range(2)]
    step = OPTICAL / depth_total
    far_side = far_ref[...] != 0
    slope = jnp.where(far_side, 1.0, -1.0) * (step / math.log(2.0) / (PAIR * UNIT))
    low, unit = colour_code(layers, depth_total)
    lx, _, lz = LIGHT_DIRECTION
    gain = DIFFUSE * lz
    scales = [(math.log(gain / scale) - low) / unit + 0.5 for scale in (PAIR * UNIT, UNIT, UNIT)]
    is_odd = (lax.axis_index("depth") & 1) == 1

    def layer(d, at):
        if 2 <= d < layers + 2:
            return x_ref[d - 2, at]
        zero, one = [ref[d % (layers + 2), at] for ref in (depth0_ref, depth1_ref)]
        return jnp.where(is_odd == (d < 2), zero, one)

    def split(pair):
        high = (pair + ROUND) - ROUND
        return high, pair - high

    def rows_of(b, h):
        return pl.ds(b * 16 + h * 8, 8)

    def look_up(b, word_ref):
        for h in range(2):
            for d in range(layers):
                index = bins_ref[d, rows_of(b, h)]
                upper = index >= HALF
                index = index & (HALF - 1)
                for p, t in enumerate(tabs):
                    word_ref[p, d, h * 8 : h * 8 + 8] = jnp.where(upper, lanes(t[1], index), lanes(t[0], index))

    def render(b, word_ref):
        at = pl.ds(b * 16, 16)
        f = [layer(d, at).astype(F32) for d in range(layers + 4)]
        for h in range(2):
            at8, rows8 = rows_of(b, h), slice(h * 8, h * 8 + 8)
            zero = jnp.zeros((8, cols), F32)
            red, green, blue, whole, total = zero, zero, zero, zero, zero
            seen = jnp.ones((8, cols), F32)
            for d in range(layers):
                gc = gc_ref[d, at8] + ge_ref[d, at8]
                light = (lx / lz) * gc + light_ref[d, at8]
                square = gc * gc + square_ref[d, at8]
                if not 2 <= d < layers - 2:
                    gd = along_depth(*[f[d + i][rows8] for i in (0, 1, 3, 4)])
                    light = light + gd
                    square = square + gd * gd
                shade = AMBIENT / gain + jnp.abs(light) * lax.rsqrt(square)
                (r, gn), (ext, bl) = [split(word_ref[p, d, rows8]) for p in range(2)]
                total = total + ext
                now = jnp.exp2(total * slope)
                weight = (now - seen) * shade
                seen = now
                red, green, blue = red + r * weight, green + gn * weight, blue + bl * weight
                whole = whole + weight
            shift = jnp.where(far_side, total * (-step / (PAIR * UNIT * unit)), 0.0)
            code = [
                (jnp.log(jnp.abs(v)) * (1.0 / unit) + (shift + scale)).astype(I32)
                for v, scale in zip((red, green + MIDDLE * whole, blue + MIDDLE * whole), scales)
            ]
            count = (total * (1.0 / PAIR) + 0.5).astype(I32)
            out_ref[b * 2 + h, 0:8, :] = code[0] + (code[1] << 16)
            out_ref[b * 2 + h, 8:16, :] = code[2] + (count << 16)

    blocks = rows // 16

    words = (even_ref, odd_ref)
    look_up(0, even_ref)
    for b in range(blocks):
        if b + 1 < blocks:
            look_up(b + 1, words[(b + 1) % 2])
        render(b, words[b % 2])


def merge_kernel(layers, depth_total, in_ref, far_ref, out_ref):
    parts, _, cols = in_ref.shape
    step = OPTICAL / depth_total / UNIT
    low, unit = colour_code(layers, depth_total)
    far_side = far_ref[...] != 0
    counts = [lax.shift_right_logical(in_ref[p, 8:16, :], 16) for p in range(parts)]
    total = counts[0]
    for v in counts[1:]:
        total = total + v
    ahead = jnp.where(far_side, total, 0)
    colour = [jnp.zeros((8, cols), F32)] * 3
    for p in range(parts):
        first, second = in_ref[p, 0:8, :], in_ref[p, 8:16, :]
        codes = [first & 0xFFFF, lax.shift_right_logical(first, 16), second & 0xFFFF]
        behind = ahead - counts[p]
        shift = jnp.where(far_side, behind, ahead).astype(F32) * -step + low
        colour = [colour[i] + jnp.exp(codes[i].astype(F32) * unit + shift) for i in range(3)]
        ahead = jnp.where(far_side, behind, ahead + counts[p])
    for i in range(3):
        out_ref[i] = colour[i]
    out_ref[3] = 1.0 - jnp.exp(total.astype(F32) * -step)


def swap(x, axis, odd):
    count = lax.axis_size(axis)
    pairs = [(i, i + 1) for i in range(odd, count - 1, 2)]
    alone = [(i, i) for i in (0, count - 1)] if odd else []
    return lax.ppermute(x, axis, pairs + [(b, a) for a, b in pairs] + alone)


def local(kernel, name, outs, *args, scratch=(), limit=16, stay=()):
    vmem, there = pl.BlockSpec(memory_space=pltpu.VMEM), pl.BlockSpec(memory_space=pltpu.HBM)
    return pl.pallas_call(
        kernel,
        out_shape=[pltpu.VMEM(s, d) for s, d in outs],
        in_specs=[there if i in stay else vmem for i in range(len(args))],
        out_specs=[vmem] * len(outs),
        scratch_shapes=list(scratch),
        compiler_params=pltpu.CompilerParams(vmem_limit_bytes=limit << 20),
        name=name,
    )(*[pltpu.with_memory_space_constraint(a, pltpu.HBM if i in stay else pltpu.VMEM) for i, a in enumerate(args)])


def on_device(density, bin_index, transfer, view_side):
    layers, rows, cols = density.shape
    count = lax.axis_size("depth")
    depth_total = layers * count
    block_rows = rows // count
    brick_f32 = ((layers, rows, cols), F32)
    faces = local(
        faces_kernel, "faces", [((2, rows, cols), BF16)] * 2, density, scratch=[pltpu.SemaphoreType.DMA((8,))], stay=(0,)
    )
    beside = [swap(faces[odd], "depth", odd) for odd in range(2)]
    (columns,) = local(columns_kernel, "columns", [((rows, cols), BF16)], density)
    beside += [swap(columns, "screen", odd) for odd in range(2)]
    side = view_side.reshape(1, cols)
    slopes = local(
        slopes_kernel,
        "slopes",
        [brick_f32] * 3
        + [((layers // 2, cols, 2 * cols), BF16), ((2, 2, 8, HALF), F32), ((8, cols), I32)],
        *(density, transfer, side),
        scratch=[pltpu.VMEM(transfer.shape, BF16), pltpu.VMEM(side.shape, I32), pltpu.SemaphoreType.DMA((2,))],
        stay=(1, 2),
    )
    (tiles,) = local(
        lambda *refs: brick_kernel(depth_total, *refs),
        "brick",
        [((count, 2 * block_rows, cols), I32)],
        *(density, *beside, bin_index, *slopes),
        scratch=[
            pltpu.VMEM(*brick_f32),
            pltpu.VMEM((2, layers, 16, cols), F32),
            pltpu.VMEM((2, layers, 16, cols), F32),
        ],
    )
    arrived = lax.all_to_all(tiles, "depth", split_axis=0, concat_axis=0, tiled=True)
    return pl.pallas_call(
        lambda *refs: merge_kernel(layers, depth_total, *refs),
        out_shape=jax.ShapeDtypeStruct((4, block_rows, cols), F32),
        in_specs=[pl.BlockSpec(memory_space=pltpu.VMEM)] * 2,
        compiler_params=pltpu.CompilerParams(vmem_limit_bytes=16 << 20),
        name="merge",
    )(*[pltpu.with_memory_space_constraint(a, pltpu.VMEM) for a in (arrived, slopes[-1])])


def solution(mesh):
    placed = (P("depth", None, "screen"), P("depth", None, "screen"), P(), P("screen"))
    return jax.shard_map(
        on_device, mesh=mesh, in_specs=placed, out_specs=P(None, "depth", "screen"), check_vma=False
    )
```

```python
import jax
import jax.numpy as jnp
from jax import lax
from jax.experimental import pallas as pl
from jax.experimental.pallas import tpu as pltpu
from jax.sharding import PartitionSpec as P
import math

LIGHT_DIRECTION = (0.36, 0.48, 0.8)
AMBIENT = 0.3
DIFFUSE = 0.7
OPTICAL = 4.0
LEAST = 0.049804688
UNIT = 4096.0
CODES = 65535.0
HALF = 128
PAIR = 4096.0
MIDDLE = 2150.0
ROUND = 1.5 * 2.0**23 * PAIR

F32, BF16, I32 = jnp.float32, jnp.bfloat16, jnp.int32


def stencil(offset):
    one = jnp.where(offset > 0, 8.0, -8.0)
    two = jnp.where(offset > 0, -1.0, 1.0)
    far = jnp.abs(offset)
    return jnp.where(far == 1, one, jnp.where(far == 2, two, 0.0)).astype(BF16)


def iota(shape, dim):
    return lax.broadcasted_iota(I32, shape, dim)


def colour_code(layers, depth_total):
    step = OPTICAL / depth_total
    low = LEAST * AMBIENT * -math.expm1(-layers * LEAST * step) * 0.999
    high = -math.expm1(-layers * step) * 1.001
    return math.log(low), math.log(high / low) / CODES


def lanes(table, index):
    numbers = lax.GatherDimensionNumbers((), (1,), (1,), (0,), (0,))
    return lax.gather(
        table, index[..., None], numbers, (1, 1), mode=lax.GatherScatterMode.PROMISE_IN_BOUNDS
    )


def along_depth(two_before, before, after, two_after):
    return 8.0 * (after - before) - (two_after - two_before)


def faces_kernel(x_hbm, first_ref, second_ref, sems):
    layers = x_hbm.shape[0]
    here, count = lax.axis_index("depth"), lax.axis_size("depth")
    odd = here & 1
    starts = [(1 - odd) * (layers - 2), odd * (layers - 2)]
    quarter = x_hbm.shape[1] // 4
    copies = [
        pltpu.make_async_copy(
            x_hbm.at[pl.ds(start, 2), pl.ds(q * quarter, quarter)], ref.at[:, pl.ds(q * quarter, quarter)], sems.at[i * 4 + q]
        )
        for i, (start, ref) in enumerate(zip(starts, (first_ref, second_ref)))
        for q in range(4)
    ]
    for copy in copies:
        copy.start()
    for copy in copies:
        copy.wait()

    @pl.when((here == 0) | (here == count - 1))
    def _():
        second_ref[...] = jnp.zeros_like(second_ref)


def columns_kernel(x_ref, cols_ref):
    layers, _, cols = x_ref.shape
    size = cols_ref.shape[0]
    k = iota((layers * cols, cols), 0)
    lane = iota((1, cols), 1) & (4 * layers - 1)
    j = lane & 3
    column = (lane >> 2) * cols + jnp.where(j < 2, j, cols - 4 + j)
    pick = jnp.where(k == column, 1.0, 0.0).astype(BF16)
    x = jnp.concatenate([x_ref[d] for d in range(layers)], axis=1)
    picked = jnp.dot(x, pick, preferred_element_type=F32)
    group = iota((size, cols), 1) // (4 * layers)
    columns = picked[:size]
    for g in range(1, cols // (4 * layers)):
        columns = jnp.where(group == g, picked[g * size : (g + 1) * size], columns)
    cols_ref[...] = columns.astype(BF16)


def slopes_kernel(x_ref, table_hbm, side_hbm, gc_ref, light_ref, square_ref, edge_ref, tabs_ref, far_ref, table_ref, side_ref, sems):
    layers, rows, cols = x_ref.shape
    copies = [
        pltpu.make_async_copy(hbm, ref, sems.at[i])
        for i, (hbm, ref) in enumerate([(table_hbm, table_ref), (side_hbm, side_ref)])
    ]
    for copy in copies:
        copy.start()
    k, c = iota((cols, cols), 0), iota((cols, cols), 1)
    inner = stencil(k - c)
    none = jnp.zeros_like(inner)
    across = stencil(iota((rows, rows), 1) - iota((rows, rows), 0))
    along = jnp.concatenate(
        [jnp.concatenate([inner, none], axis=1), jnp.concatenate([none, inner], axis=1)], axis=0
    )
    ly, lz = LIGHT_DIRECTION[1:]
    for d in range(0, layers, 2):
        x = jnp.concatenate([x_ref[d], x_ref[d + 1]], axis=1)
        gc = jnp.dot(x, along, preferred_element_type=F32)
        gr = jnp.dot(across, x, preferred_element_type=F32)
        for e in range(d, d + 2):
            at = slice((e - d) * cols, (e - d + 1) * cols)
            gc_ref[e] = gc[:, at]
            light = (ly / lz) * gr[:, at]
            square = gr[:, at] * gr[:, at] + 144.0
            if 2 <= e < layers - 2:
                gd = along_depth(*[x_ref[e + i].astype(F32) for i in (-2, -1, 1, 2)])
                light = light + gd
                square = square + gd * gd
            light_ref[e] = light
            square_ref[e] = square
    j = k & 3
    outer = stencil(jnp.where(j < 2, cols + j, j - 4) - c)
    for d in range(layers):
        edge_ref[d // 2, :, (d % 2) * cols : (d % 2 + 1) * cols] = jnp.where((k & (4 * layers - 1)) >> 2 == d, outer, none)
    for copy in copies:
        copy.wait()
    far_ref[...] = jnp.broadcast_to(side_ref[...], far_ref.shape)
    table = table_ref[...].astype(F32) * UNIT
    for p, (high, low) in enumerate([(0, 1), (3, 2)]):
        pair = table[high : high + 1] * PAIR + (table[low : low + 1] - MIDDLE)
        for h in range(2):
            tabs_ref[p, h] = jnp.broadcast_to(pair[:, h * HALF : (h + 1) * HALF], (8, HALF))


def outer_slopes(first_ref, second_ref, edge_ref, ge_ref):
    layers, rows, cols = ge_ref.shape
    here, count = lax.axis_index("screen"), lax.axis_size("screen")
    outermost = jnp.where((here == 0) | (here == count - 1), 2, 0)
    lane = iota(first_ref.shape, 1)
    source = (((lane >> 1) & 1) ^ (here & 1)) + outermost
    first, second = first_ref[...], second_ref[...]
    none = jnp.zeros_like(second)
    halo = jnp.where((source & 1) == 0, first, jnp.where(source == 1, second, none))
    groups = range(cols // (4 * layers))
    halo = jnp.concatenate([jnp.where(lane // (4 * layers) == g, halo, none) for g in groups], axis=0)
    for d in range(0, layers, 2):
        ge = jnp.dot(halo, edge_ref[d // 2], preferred_element_type=F32)
        for i in range(2):
            ge_ref[d + i] = ge[:, i * cols : (i + 1) * cols]


def brick_kernel(depth_total, x_ref, depth1_ref, depth0_ref, screen1_ref, screen0_ref, bins_ref, gc_ref, light_ref, square_ref, edge_ref, tabs_ref, far_ref, out_ref, ge_ref, even_ref, odd_ref):
    layers, rows, cols = x_ref.shape
    outer_slopes(screen0_ref, screen1_ref, edge_ref, ge_ref)
    tabs = [[tabs_ref[p, h] for h in range(2)] for p in range(2)]
    step = OPTICAL / depth_total
    far_side = far_ref[...] != 0
    slope = jnp.where(far_side, 1.0, -1.0) * (step / math.log(2.0) / (PAIR * UNIT))
    low, unit = colour_code(layers, depth_total)
    lx, _, lz = LIGHT_DIRECTION
    gain = DIFFUSE * lz
    scales = [(math.log(gain / scale) - low) / unit + 0.5 for scale in (PAIR * UNIT, UNIT, UNIT)]
    is_odd = (lax.axis_index("depth") & 1) == 1

    def layer(d, at):
        if 2 <= d < layers + 2:
            return x_ref[d - 2, at]
        zero, one = [ref[d % (layers + 2), at] for ref in (depth0_ref, depth1_ref)]
        return jnp.where(is_odd == (d < 2), zero, one)

    def split(pair):
        high = (pair + ROUND) - ROUND
        return high, pair - high

    def rows_of(b, h):
        return pl.ds(b * 16 + h * 8, 8)

    def look_up(b, word_ref):
        for h in range(2):
            for d in range(layers):
                index = bins_ref[d, rows_of(b, h)]
                upper = index >= HALF
                index = index & (HALF - 1)
                for p, t in enumerate(tabs):
                    word_ref[p, d, h * 8 : h * 8 + 8] = jnp.where(upper, lanes(t[1], index), lanes(t[0], index))

    def render(b, word_ref):
        at = pl.ds(b * 16, 16)
        f = [layer(d, at).astype(F32) for d in range(layers + 4)]
        for h in range(2):
            at8, rows8 = rows_of(b, h), slice(h * 8, h * 8 + 8)
            zero = jnp.zeros((8, cols), F32)
            red, green, blue, whole, total = zero, zero, zero, zero, zero
            seen = jnp.ones((8, cols), F32)
            for d in range(layers):
                gc = gc_ref[d, at8] + ge_ref[d, at8]
                light = (lx / lz) * gc + light_ref[d, at8]
                square = gc * gc + square_ref[d, at8]
                if not 2 <= d < layers - 2:
                    gd = along_depth(*[f[d + i][rows8] for i in (0, 1, 3, 4)])
                    light = light + gd
                    square = square + gd * gd
                shade = AMBIENT / gain + jnp.abs(light) * lax.rsqrt(square)
                (r, gn), (ext, bl) = [split(word_ref[p, d, rows8]) for p in range(2)]
                total = total + ext
                now = jnp.exp2(total * slope)
                weight = (now - seen) * shade
                seen = now
                red, green, blue = red + r * weight, green + gn * weight, blue + bl * weight
                whole = whole + weight
            shift = jnp.where(far_side, total * (-step / (PAIR * UNIT * unit)), 0.0)
            code = [
                (jnp.log(jnp.abs(v)) * (1.0 / unit) + (shift + scale)).astype(I32)
                for v, scale in zip((red, green + MIDDLE * whole, blue + MIDDLE * whole), scales)
            ]
            count = (total * (1.0 / PAIR) + 0.5).astype(I32)
            out_ref[b * 2 + h, 0:8, :] = code[0] + (code[1] << 16)
            out_ref[b * 2 + h, 8:16, :] = code[2] + (count << 16)

    blocks = rows // 16

    words = (even_ref, odd_ref)
    look_up(0, even_ref)
    for b in range(blocks):
        if b + 1 < blocks:
            look_up(b + 1, words[(b + 1) % 2])
        render(b, words[b % 2])


def merge_kernel(layers, depth_total, in_ref, far_ref, out_ref):
    parts, _, cols = in_ref.shape
    step = OPTICAL / depth_total / UNIT
    low, unit = colour_code(layers, depth_total)
    far_side = far_ref[...] != 0
    counts = [lax.shift_right_logical(in_ref[p, 8:16, :], 16) for p in range(parts)]
    total = counts[0]
    for v in counts[1:]:
        total = total + v
    ahead = jnp.where(far_side, total, 0)
    colour = [jnp.zeros((8, cols), F32)] * 3
    for p in range(parts):
        first, second = in_ref[p, 0:8, :], in_ref[p, 8:16, :]
        codes = [first & 0xFFFF, lax.shift_right_logical(first, 16), second & 0xFFFF]
        behind = ahead - counts[p]
        shift = jnp.where(far_side, behind, ahead).astype(F32) * -step + low
        colour = [colour[i] + jnp.exp(codes[i].astype(F32) * unit + shift) for i in range(3)]
        ahead = jnp.where(far_side, behind, ahead + counts[p])
    for i in range(3):
        out_ref[i] = colour[i]
    out_ref[3] = 1.0 - jnp.exp(total.astype(F32) * -step)


def swap(x, axis, odd):
    count = lax.axis_size(axis)
    pairs = [(i, i + 1) for i in range(odd, count - 1, 2)]
    alone = [(i, i) for i in (0, count - 1)] if odd else []
    return lax.ppermute(x, axis, pairs + [(b, a) for a, b in pairs] + alone)


def local(kernel, name, outs, *args, scratch=(), limit=16, stay=()):
    vmem, there = pl.BlockSpec(memory_space=pltpu.VMEM), pl.BlockSpec(memory_space=pltpu.HBM)
    return pl.pallas_call(
        kernel,
        out_shape=[pltpu.VMEM(s, d) for s, d in outs],
        in_specs=[there if i in stay else vmem for i in range(len(args))],
        out_specs=[vmem] * len(outs),
        scratch_shapes=list(scratch),
        compiler_params=pltpu.CompilerParams(vmem_limit_bytes=limit << 20),
        name=name,
    )(*[pltpu.with_memory_space_constraint(a, pltpu.HBM if i in stay else pltpu.VMEM) for i, a in enumerate(args)])


def on_device(density, bin_index, transfer, view_side):
    layers, rows, cols = density.shape
    count = lax.axis_size("depth")
    depth_total = layers * count
    block_rows = rows // count
    brick_f32 = ((layers, rows, cols), F32)
    faces = local(
        faces_kernel, "faces", [((2, rows, cols), BF16)] * 2, density, scratch=[pltpu.SemaphoreType.DMA((8,))], stay=(0,)
    )
    beside = [swap(faces[odd], "depth", odd) for odd in range(2)]
    (columns,) = local(columns_kernel, "columns", [((rows * 4 * layers // cols, cols), BF16)], density)
    beside += [swap(columns, "screen", odd) for odd in range(2)]
    side = view_side.reshape(1, cols)
    slopes = local(
        slopes_kernel,
        "slopes",
        [brick_f32] * 3
        + [((layers // 2, cols, 2 * cols), BF16), ((2, 2, 8, HALF), F32), ((8, cols), I32)],
        *(density, transfer, side),
        scratch=[pltpu.VMEM(transfer.shape, BF16), pltpu.VMEM(side.shape, I32), pltpu.SemaphoreType.DMA((2,))],
        stay=(1, 2),
    )
    (tiles,) = local(
        lambda *refs: brick_kernel(depth_total, *refs),
        "brick",
        [((count, 2 * block_rows, cols), I32)],
        *(density, beside[1], beside[0], beside[3], beside[2], bin_index, *slopes),
        scratch=[
            pltpu.VMEM(*brick_f32),
            pltpu.VMEM((2, layers, 16, cols), F32),
            pltpu.VMEM((2, layers, 16, cols), F32),
        ],
    )
    arrived = lax.all_to_all(tiles, "depth", split_axis=0, concat_axis=0, tiled=True)
    return pl.pallas_call(
        lambda *refs: merge_kernel(layers, depth_total, *refs),
        out_shape=jax.ShapeDtypeStruct((4, block_rows, cols), F32),
        in_specs=[pl.BlockSpec(memory_space=pltpu.VMEM)] * 2,
        compiler_params=pltpu.CompilerParams(vmem_limit_bytes=16 << 20),
        name="merge",
    )(*[pltpu.with_memory_space_constraint(a, pltpu.VMEM) for a in (arrived, slopes[-1])])


def solution(mesh):
    placed = (P("depth", None, "screen"), P("depth", None, "screen"), P(), P("screen"))
    return jax.shard_map(
        on_device, mesh=mesh, in_specs=placed, out_specs=P(None, "depth", "screen"), check_vma=False
    )
```

```python
import jax
import jax.numpy as jnp
from jax import lax
from jax.experimental import pallas as pl
from jax.experimental.pallas import tpu as pltpu
from jax.sharding import PartitionSpec as P
import math

LIGHT_DIRECTION = (0.36, 0.48, 0.8)
AMBIENT = 0.3
DIFFUSE = 0.7
OPTICAL = 4.0
LEAST = 0.049804688
UNIT = 4096.0
CODES = 65535.0
EARLY = 3
HALF = 128
PAIR = 4096.0
MIDDLE = 2150.0
ROUND = 1.5 * 2.0**23 * PAIR

F32, BF16, I32 = jnp.float32, jnp.bfloat16, jnp.int32


def stencil(offset):
    one = jnp.where(offset > 0, 8.0, -8.0)
    two = jnp.where(offset > 0, -1.0, 1.0)
    far = jnp.abs(offset)
    return jnp.where(far == 1, one, jnp.where(far == 2, two, 0.0)).astype(BF16)


def iota(shape, dim):
    return lax.broadcasted_iota(I32, shape, dim)


def colour_code(layers, depth_total):
    step = OPTICAL / depth_total
    low = LEAST * AMBIENT * -math.expm1(-layers * LEAST * step) * 0.999
    high = -math.expm1(-layers * step) * 1.001
    return math.log(low), math.log(high / low) / CODES


def lanes(table, index):
    numbers = lax.GatherDimensionNumbers((), (1,), (1,), (0,), (0,))
    return lax.gather(
        table, index[..., None], numbers, (1, 1), mode=lax.GatherScatterMode.PROMISE_IN_BOUNDS
    )


def along_depth(two_before, before, after, two_after):
    return 8.0 * (after - before) - (two_after - two_before)


def faces_kernel(x_hbm, first_ref, second_ref, sems):
    layers = x_hbm.shape[0]
    here, count = lax.axis_index("depth"), lax.axis_size("depth")
    odd = here & 1
    starts = [(1 - odd) * (layers - 2), odd * (layers - 2)]
    quarter = x_hbm.shape[1] // 4
    copies = [
        pltpu.make_async_copy(
            x_hbm.at[pl.ds(start, 2), pl.ds(q * quarter, quarter)], ref.at[:, pl.ds(q * quarter, quarter)], sems.at[i * 4 + q]
        )
        for i, (start, ref) in enumerate(zip(starts, (first_ref, second_ref)))
        for q in range(4)
    ]
    for copy in copies:
        copy.start()
    for copy in copies:
        copy.wait()

    @pl.when((here == 0) | (here == count - 1))
    def _():
        second_ref[...] = jnp.zeros_like(second_ref)


def columns_kernel(x_ref, cols_ref):
    layers, _, cols = x_ref.shape
    size = cols_ref.shape[0]
    k = iota((layers * cols, cols), 0)
    lane = iota((1, cols), 1) & (4 * layers - 1)
    j = lane & 3
    column = (lane >> 2) * cols + jnp.where(j < 2, j, cols - 4 + j)
    pick = jnp.where(k == column, 1.0, 0.0).astype(BF16)
    x = jnp.concatenate([x_ref[d] for d in range(layers)], axis=1)
    picked = jnp.dot(x, pick, preferred_element_type=F32)
    group = iota((size, cols), 1) // (4 * layers)
    columns = picked[:size]
    for g in range(1, cols // (4 * layers)):
        columns = jnp.where(group == g, picked[g * size : (g + 1) * size], columns)
    cols_ref[...] = columns.astype(BF16)


def look_up(tabs, bins_ref, base, word_ref, to):
    for h in (0, 8):
        for d in range(bins_ref.shape[0]):
            index = bins_ref[d, base + h : base + h + 8]
            upper = index >= HALF
            index = index & (HALF - 1)
            for p, t in enumerate(tabs):
                word_ref[p, d, to + h : to + h + 8] = jnp.where(upper, lanes(t[1], index), lanes(t[0], index))


def slopes_kernel(x_ref, table_hbm, side_hbm, bins_hbm, gc_ref, light_ref, square_ref, edge_ref, tabs_ref, far_ref, word_ref, table_ref, side_ref, bins_ref, sems):
    layers, rows, cols = x_ref.shape
    copies = [
        pltpu.make_async_copy(hbm, ref, sems.at[i])
        for i, (hbm, ref) in enumerate([(table_hbm, table_ref), (side_hbm, side_ref), (bins_hbm.at[:, pl.ds(0, 16 * EARLY)], bins_ref)])
    ]
    for copy in copies:
        copy.start()
    k, c = iota((cols, cols), 0), iota((cols, cols), 1)
    inner = stencil(k - c)
    none = jnp.zeros_like(inner)
    across = stencil(iota((rows, rows), 1) - iota((rows, rows), 0))
    along = jnp.concatenate(
        [jnp.concatenate([inner, none], axis=1), jnp.concatenate([none, inner], axis=1)], axis=0
    )
    ly, lz = LIGHT_DIRECTION[1:]
    for d in range(0, layers, 2):
        x = jnp.concatenate([x_ref[d], x_ref[d + 1]], axis=1)
        gc = jnp.dot(x, along, preferred_element_type=F32)
        gr = jnp.dot(across, x, preferred_element_type=F32)
        for e in range(d, d + 2):
            at = slice((e - d) * cols, (e - d + 1) * cols)
            gc_ref[e] = gc[:, at]
            light = (ly / lz) * gr[:, at]
            square = gr[:, at] * gr[:, at] + 144.0
            if 2 <= e < layers - 2:
                gd = along_depth(*[x_ref[e + i].astype(F32) for i in (-2, -1, 1, 2)])
                light = light + gd
                square = square + gd * gd
            light_ref[e] = light
            square_ref[e] = square
        if d == 0:
            for copy in copies:
                copy.wait()
            far_ref[...] = jnp.broadcast_to(side_ref[...], far_ref.shape)
            table = table_ref[...].astype(F32) * UNIT
            for p, (high, low) in enumerate([(0, 1), (3, 2)]):
                pair = table[high : high + 1] * PAIR + (table[low : low + 1] - MIDDLE)
                for h in range(2):
                    tabs_ref[p, h] = jnp.broadcast_to(pair[:, h * HALF : (h + 1) * HALF], (8, HALF))
            tabs = [[tabs_ref[p, h] for h in range(2)] for p in range(2)]
        elif d // 2 <= EARLY:
            look_up(tabs, bins_ref, (d // 2 - 1) * 16, word_ref, (d // 2 - 1) * 16)
    j = k & 3
    outer = stencil(jnp.where(j < 2, cols + j, j - 4) - c)
    for d in range(layers):
        edge_ref[d // 2, :, (d % 2) * cols : (d % 2 + 1) * cols] = jnp.where((k & (4 * layers - 1)) >> 2 == d, outer, none)


def outer_slopes(first_ref, second_ref, edge_ref, ge_ref):
    layers, rows, cols = ge_ref.shape
    here, count = lax.axis_index("screen"), lax.axis_size("screen")
    outermost = jnp.where((here == 0) | (here == count - 1), 2, 0)
    lane = iota(first_ref.shape, 1)
    source = (((lane >> 1) & 1) ^ (here & 1)) + outermost
    first, second = first_ref[...], second_ref[...]
    none = jnp.zeros_like(second)
    halo = jnp.where((source & 1) == 0, first, jnp.where(source == 1, second, none))
    groups = range(cols // (4 * layers))
    halo = jnp.concatenate([jnp.where(lane // (4 * layers) == g, halo, none) for g in groups], axis=0)
    for d in range(0, layers, 2):
        ge = jnp.dot(halo, edge_ref[d // 2], preferred_element_type=F32)
        for i in range(2):
            ge_ref[d + i] = ge[:, i * cols : (i + 1) * cols]


def brick_kernel(depth_total, x_ref, depth1_ref, depth0_ref, screen1_ref, screen0_ref, bins_ref, gc_ref, light_ref, square_ref, edge_ref, tabs_ref, far_ref, early_ref, out_ref, ge_ref, even_ref, odd_ref):
    layers, rows, cols = x_ref.shape
    outer_slopes(screen0_ref, screen1_ref, edge_ref, ge_ref)
    tabs = [[tabs_ref[p, h] for h in range(2)] for p in range(2)]
    step = OPTICAL / depth_total
    far_side = far_ref[...] != 0
    slope = jnp.where(far_side, 1.0, -1.0) * (step / math.log(2.0) / (PAIR * UNIT))
    low, unit = colour_code(layers, depth_total)
    lx, _, lz = LIGHT_DIRECTION
    gain = DIFFUSE * lz
    scales = [(math.log(gain / scale) - low) / unit + 0.5 for scale in (PAIR * UNIT, UNIT, UNIT)]
    is_odd = (lax.axis_index("depth") & 1) == 1

    def layer(d, at):
        if 2 <= d < layers + 2:
            return x_ref[d - 2, at]
        zero, one = [ref[d % (layers + 2), at] for ref in (depth0_ref, depth1_ref)]
        return jnp.where(is_odd == (d < 2), zero, one)

    def split(pair):
        high = (pair + ROUND) - ROUND
        return high, pair - high

    def rows_of(b, h):
        return pl.ds(b * 16 + h * 8, 8)

    def render(b, word_ref, to):
        at = pl.ds(b * 16, 16)
        f = [layer(d, at).astype(F32) for d in range(layers + 4)]
        for h in range(2):
            at8, rows8 = rows_of(b, h), slice(h * 8, h * 8 + 8)
            zero = jnp.zeros((8, cols), F32)
            red, green, blue, whole, total = zero, zero, zero, zero, zero
            seen = jnp.ones((8, cols), F32)
            for d in range(layers):
                gc = gc_ref[d, at8] + ge_ref[d, at8]
                light = (lx / lz) * gc + light_ref[d, at8]
                square = gc * gc + square_ref[d, at8]
                if not 2 <= d < layers - 2:
                    gd = along_depth(*[f[d + i][rows8] for i in (0, 1, 3, 4)])
                    light = light + gd
                    square = square + gd * gd
                shade = AMBIENT / gain + jnp.abs(light) * lax.rsqrt(square)
                (r, gn), (ext, bl) = [split(word_ref[p, d, to + h * 8 : to + h * 8 + 8]) for p in range(2)]
                total = total + ext
                now = jnp.exp2(total * slope)
                weight = (now - seen) * shade
                seen = now
                red, green, blue = red + r * weight, green + gn * weight, blue + bl * weight
                whole = whole + weight
            shift = jnp.where(far_side, total * (-step / (PAIR * UNIT * unit)), 0.0)
            code = [
                (jnp.log(jnp.abs(v)) * (1.0 / unit) + (shift + scale)).astype(I32)
                for v, scale in zip((red, green + MIDDLE * whole, blue + MIDDLE * whole), scales)
            ]
            count = (total * (1.0 / PAIR) + 0.5).astype(I32)
            out_ref[b * 2 + h, 0:8, :] = code[0] + (code[1] << 16)
            out_ref[b * 2 + h, 8:16, :] = code[2] + (count << 16)

    blocks = rows // 16

    words = (even_ref, odd_ref)
    for b in range(blocks):
        if EARLY <= b + 1 < blocks:
            look_up(tabs, bins_ref, (b + 1) * 16, words[(b + 1) % 2], 0)
        if b < EARLY:
            render(b, early_ref, b * 16)
        else:
            render(b, words[b % 2], 0)


def merge_kernel(layers, depth_total, in_ref, far_ref, out_ref):
    parts, _, cols = in_ref.shape
    step = OPTICAL / depth_total / UNIT
    low, unit = colour_code(layers, depth_total)
    far_side = far_ref[...] != 0
    counts = [lax.shift_right_logical(in_ref[p, 8:16, :], 16) for p in range(parts)]
    total = counts[0]
    for v in counts[1:]:
        total = total + v
    ahead = jnp.where(far_side, total, 0)
    colour = [jnp.zeros((8, cols), F32)] * 3
    for p in range(parts):
        first, second = in_ref[p, 0:8, :], in_ref[p, 8:16, :]
        codes = [first & 0xFFFF, lax.shift_right_logical(first, 16), second & 0xFFFF]
        behind = ahead - counts[p]
        shift = jnp.where(far_side, behind, ahead).astype(F32) * -step + low
        colour = [colour[i] + jnp.exp(codes[i].astype(F32) * unit + shift) for i in range(3)]
        ahead = jnp.where(far_side, behind, ahead + counts[p])
    for i in range(3):
        out_ref[i] = colour[i]
    out_ref[3] = 1.0 - jnp.exp(total.astype(F32) * -step)


def swap(x, axis, odd):
    count = lax.axis_size(axis)
    pairs = [(i, i + 1) for i in range(odd, count - 1, 2)]
    alone = [(i, i) for i in (0, count - 1)] if odd else []
    return lax.ppermute(x, axis, pairs + [(b, a) for a, b in pairs] + alone)


def local(kernel, name, outs, *args, scratch=(), limit=16, stay=()):
    vmem, there = pl.BlockSpec(memory_space=pltpu.VMEM), pl.BlockSpec(memory_space=pltpu.HBM)
    return pl.pallas_call(
        kernel,
        out_shape=[pltpu.VMEM(s, d) for s, d in outs],
        in_specs=[there if i in stay else vmem for i in range(len(args))],
        out_specs=[vmem] * len(outs),
        scratch_shapes=list(scratch),
        compiler_params=pltpu.CompilerParams(vmem_limit_bytes=limit << 20),
        name=name,
    )(*[pltpu.with_memory_space_constraint(a, pltpu.HBM if i in stay else pltpu.VMEM) for i, a in enumerate(args)])


def on_device(density, bin_index, transfer, view_side):
    layers, rows, cols = density.shape
    count = lax.axis_size("depth")
    depth_total = layers * count
    block_rows = rows // count
    brick_f32 = ((layers, rows, cols), F32)
    faces = local(
        faces_kernel, "faces", [((2, rows, cols), BF16)] * 2, density, scratch=[pltpu.SemaphoreType.DMA((8,))], stay=(0,)
    )
    beside = [swap(faces[odd], "depth", odd) for odd in range(2)]
    (columns,) = local(columns_kernel, "columns", [((rows * 4 * layers // cols, cols), BF16)], density)
    beside += [swap(columns, "screen", odd) for odd in range(2)]
    side = view_side.reshape(1, cols)
    slopes = local(
        slopes_kernel,
        "slopes",
        [brick_f32] * 3
        + [((layers // 2, cols, 2 * cols), BF16), ((2, 2, 8, HALF), F32), ((8, cols), I32), ((2, layers, 16 * EARLY, cols), F32)],
        *(density, transfer, side, bin_index),
        scratch=[pltpu.VMEM(transfer.shape, BF16), pltpu.VMEM(side.shape, I32), pltpu.VMEM((layers, 16 * EARLY, cols), I32), pltpu.SemaphoreType.DMA((3,))],
        stay=(1, 2, 3),
    )
    (tiles,) = local(
        lambda *refs: brick_kernel(depth_total, *refs),
        "brick",
        [((count, 2 * block_rows, cols), I32)],
        *(density, beside[1], beside[0], beside[3], beside[2], bin_index, *slopes),
        scratch=[
            pltpu.VMEM(*brick_f32),
            pltpu.VMEM((2, layers, 16, cols), F32),
            pltpu.VMEM((2, layers, 16, cols), F32),
        ],
    )
    arrived = lax.all_to_all(tiles, "depth", split_axis=0, concat_axis=0, tiled=True)
    return pl.pallas_call(
        lambda *refs: merge_kernel(layers, depth_total, *refs),
        out_shape=jax.ShapeDtypeStruct((4, block_rows, cols), F32),
        in_specs=[pl.BlockSpec(memory_space=pltpu.VMEM)] * 2,
        compiler_params=pltpu.CompilerParams(vmem_limit_bytes=16 << 20),
        name="merge",
    )(*[pltpu.with_memory_space_constraint(a, pltpu.VMEM) for a in (arrived, slopes[-2])])


def solution(mesh):
    placed = (P("depth", None, "screen"), P("depth", None, "screen"), P(), P("screen"))
    return jax.shard_map(
        on_device, mesh=mesh, in_specs=placed, out_specs=P(None, "depth", "screen"), check_vma=False
    )
```
